128 devices in a mesh: row: 16 (over x, z), col: 8 (over y, core).
Axes of the slice: x: 4, y: 4, z: 4, core: 2. Of those that a mesh axis runs over, the one named last changes fastest.
Arguments:
- initial_estimate0: float32 [96, 256, 2048], P(None, 'row', 'col'), may hold values from 0.1 to 1
- clutter: float32 [256, 2048], P('row', 'col'), may hold values from 0 to 1.5
- counts: int32 [128, 96, 128], P(('row', 'col')), may hold values from 1 to 10000
- antenna_settings: float32 [128, 5, 128], P(('row', 'col')), as said below
- tile_block_list: int32 [16, 8, 32], P('row', 'col'), may hold values from 0 to 127, as said below
- tile_block_count: int32 [16, 8], P('row', 'col'), may hold values from 1 to 32
Outputs:
- estimate: float32 [96, 256, 2048], P(None, 'row', 'col')
The draws below stay inside these ranges and needn't reach their ends.
Inputs may be any that keep to these rules, and one draw needn't show every extreme that they name: `tile_block_list`: block b's owner group along row is b // 8; entry i of a tile's list is used only when i < tile_block_count, and unused entries hold 0; the listed blocks of one tile are distinct; every block is listed by some tile; one tile lists at most 2 blocks of one owner group, and the tiles of some column list 32 blocks each. `antenna_settings`: radii and gains are positive.
All inputs are finite; a program needn't handle non-finite values.
Results may differ from the reference program's by a relative error of at most 0.0003.
Values sent between devices are 32-bit elements; how exact they have to be, the bound alone decides.
No kernel may reach another device: no remote copies, remote signals or barrier semaphores. Data moves between devices by JAX's collectives and lax.ppermute only.
A program may use at most 64 MiB of HBM per device.

```python
import math
import jax
import jax.numpy as jnp
from jax import lax

QUARTER_MAPS = 96
TR = 16
TC = 256
BLOCK_ANTENNAS = 128
TILE_BLOCK_LIMIT = 32
ITERS = 2
GR = 256
GC = 2048
ANTENNA_BLOCKS = 128
N_ROW = 16
N_COL = 8


def list_parts(key):
    base = jax.random.randint(jax.random.fold_in(key, 11), (N_ROW, N_COL), TILE_BLOCK_LIMIT // 4, TILE_BLOCK_LIMIT // 2 + 1)
    full_col = jax.random.randint(jax.random.fold_in(key, 12), (), 0, N_COL)
    columns = jnp.arange(N_COL, dtype=jnp.int32)[None, :]
    listed = jnp.where(columns == full_col, TILE_BLOCK_LIMIT, base).astype(jnp.int32)
    tile_index = jnp.arange(N_ROW, dtype=jnp.int32)[:, None] * N_COL + columns
    first = jnp.clip(tile_index - listed // 2, 0, N_ROW * N_COL - listed)
    slots = jnp.arange(TILE_BLOCK_LIMIT, dtype=jnp.int32)
    spatial = first[:, :, None] + slots[None, None, :]
    block_numbers = spatial % N_ROW * N_COL + spatial // N_ROW
    block_numbers = jnp.where(slots[None, None, :] < listed[:, :, None], block_numbers, 0)
    return (listed, block_numbers.astype(jnp.int32))


def draw_tile_block_list(key, part):
    return list_parts(jax.random.fold_in(key, 5))[1]


def draw_tile_block_count(key, part):
    return list_parts(jax.random.fold_in(key, 5))[0]


def draw_antenna_settings(key, part):
    blocks = jnp.arange(ANTENNA_BLOCKS, dtype=jnp.int32)
    spatial = blocks % N_COL * N_ROW + blocks // N_COL
    home_row = (spatial // N_COL).astype(jnp.float32)
    home_col = (spatial % N_COL).astype(jnp.float32)
    row_shift = jax.random.uniform(jax.random.fold_in(key, 21), (ANTENNA_BLOCKS, BLOCK_ANTENNAS), jnp.float32, -1.0, 2.0)
    column_shift = jax.random.uniform(jax.random.fold_in(key, 22), (ANTENNA_BLOCKS, BLOCK_ANTENNAS), jnp.float32, -0.5, 1.5)
    position_row = (home_row[:, None] + row_shift) * TR
    position_column = (home_col[:, None] + column_shift) * TC
    antenna_radius = jnp.exp(jax.random.uniform(jax.random.fold_in(key, 23), (ANTENNA_BLOCKS, BLOCK_ANTENNAS), jnp.float32, jnp.log(16.0), jnp.log(256.0)))
    antenna_gain = jnp.exp(jax.random.uniform(jax.random.fold_in(key, 24), (ANTENNA_BLOCKS, BLOCK_ANTENNAS), jnp.float32, jnp.log(0.5), jnp.log(2.0)))
    antenna_group = jax.random.uniform(jax.random.fold_in(key, 25), (ANTENNA_BLOCKS, BLOCK_ANTENNAS), jnp.float32, 0.5, 2.0)
    return jnp.stack([position_row, position_column, antenna_radius, antenna_gain, antenna_group], axis=1).astype(jnp.float32)


def plant(drawn, rng, smallest, high):
    place = [jax.random.randint(jax.random.fold_in(rng, axis), (), 0, length) for axis, length in enumerate(drawn.shape)]
    widest = drawn.shape.index(max(drawn.shape))
    beside = place[:widest] + [(place[widest] + 1) % drawn.shape[widest]] + place[widest + 1:]
    return drawn.at[tuple(place)].set(smallest).at[tuple(beside)].set(high)


def steps_of(rng, dims, cuts, smallest, high):
    gain, own = 1.0, jax.random.fold_in(rng, 6)
    for dim, shards_of in cuts:
        steps = jnp.exp(jax.random.uniform(jax.random.fold_in(own, dim), (shards_of,), jnp.float32, smallest / len(cuts), high / len(cuts)))
        gain = gain * jnp.repeat(steps, dims[dim] // shards_of).reshape([-1 if axis == dim else 1 for axis in range(len(dims))])
    return gain


def setup_inputs(seed: int = 0) -> dict:
    seeds = jax.random.split(jax.random.key(seed), 7)
    initial_estimate0 = jnp.clip(jnp.exp(math.log(1.0) - 2.3025851 * jax.random.uniform(seeds[0], (QUARTER_MAPS, GR, GC), jnp.float32) ** steps_of(seeds[0], (QUARTER_MAPS, GR, GC), ((1, 16), (2, 8)), -0.2, 0.2)), 0.1, 1.0)
    clutter = jnp.clip(1.5 * jax.random.uniform(seeds[1], (GR, GC), jnp.float32) ** steps_of(seeds[1], (GR, GC), ((0, 16), (1, 8)), -0.2, 0.2), 0.0, 1.5)
    counts = plant(jax.random.randint(seeds[2], (ANTENNA_BLOCKS, QUARTER_MAPS, BLOCK_ANTENNAS), 1, 10001), jax.random.fold_in(seeds[2], 1), 1, 10000).astype(jnp.int32)
    antenna_settings = draw_antenna_settings(jax.random.fold_in(seeds[6], 71), 0)
    tile_block_list = draw_tile_block_list(jax.random.fold_in(seeds[6], 71), 0)
    tile_block_count = draw_tile_block_count(jax.random.fold_in(seeds[6], 71), 0)
    return dict(initial_estimate0=initial_estimate0, clutter=clutter, counts=counts, antenna_settings=antenna_settings, tile_block_list=tile_block_list, tile_block_count=tile_block_count)


def coverage(settings_rows, terrain_loss, pixel_row, pixel_column):
    antenna_row = settings_rows[:, 0, :, None]
    antenna_column = settings_rows[:, 1, :, None]
    antenna_radius = settings_rows[:, 2, :, None]
    antenna_gain = settings_rows[:, 3, :, None]
    antenna_group = settings_rows[:, 4, :, None]
    row_distance = pixel_row[None, None, :] - antenna_row
    column_distance = pixel_column[None, None, :] - antenna_column
    return antenna_gain * jnp.exp(-antenna_group * terrain_loss[None, None, :]) / (1.0 + (row_distance * row_distance + column_distance * column_distance) / (antenna_radius * antenna_radius))


def tile_coverage(tile_index, clutter, antenna_settings, flattened_lists, flattened_counts):
    tile_row = tile_index // N_COL
    tile_col = tile_index % N_COL
    local_row = jnp.repeat(jnp.arange(TR, dtype=jnp.int32), TC)
    local_col = jnp.tile(jnp.arange(TC, dtype=jnp.int32), TR)
    pixel_row = (tile_row * TR + local_row).astype(jnp.float32) + 0.5
    pixel_column = (tile_col * TC + local_col).astype(jnp.float32) + 0.5
    terrain_loss = lax.dynamic_slice(clutter, ((tile_row * TR).astype(jnp.int32), (tile_col * TC).astype(jnp.int32)), (TR, TC)).reshape(TR * TC)
    block_numbers = flattened_lists[tile_index]
    slot_live = (jnp.arange(TILE_BLOCK_LIMIT, dtype=jnp.int32) < flattened_counts[tile_index]).astype(jnp.float32)
    settings_rows = antenna_settings[block_numbers]
    return coverage(settings_rows, terrain_loss, pixel_row, pixel_column) * slot_live[:, None, None]


def reference(initial_estimate0, clutter, counts, antenna_settings, tile_block_list, tile_block_count):
    tile_count = N_ROW * N_COL
    n_pixels = TR * TC
    est_tiles = initial_estimate0.reshape(QUARTER_MAPS, N_ROW, TR, N_COL, TC).transpose(1, 3, 0, 2, 4).reshape(tile_count, QUARTER_MAPS, n_pixels)
    flattened_lists = tile_block_list.reshape(tile_count, TILE_BLOCK_LIMIT)
    flattened_counts = tile_block_count.reshape(tile_count)
    tile_ids = jnp.arange(tile_count, dtype=jnp.int32)
    highest = lax.Precision.HIGHEST

    def forward_first(args):
        tile_index, estimate = args
        coverage_value = tile_coverage(tile_index, clutter, antenna_settings, flattened_lists, flattened_counts)
        partial_value = jnp.einsum('tp,sap->sta', estimate, coverage_value, precision=highest)
        return partial_value, jnp.sum(coverage_value, axis=(0, 1))

    def forward(args):
        tile_index, estimate = args
        coverage_value = tile_coverage(tile_index, clutter, antenna_settings, flattened_lists, flattened_counts)
        return jnp.einsum('tp,sap->sta', estimate, coverage_value, precision=highest)

    sensitivity = None
    for sweep in range(ITERS):
        if sweep == 0:
            partial_sums, sensitivity = lax.map(forward_first, (tile_ids, est_tiles))
        else:
            partial_sums = lax.map(forward, (tile_ids, est_tiles))
        projected_counts = jnp.zeros((ANTENNA_BLOCKS, QUARTER_MAPS, BLOCK_ANTENNAS), jnp.float32).at[flattened_lists.reshape(-1)].add(partial_sums.reshape(tile_count * TILE_BLOCK_LIMIT, QUARTER_MAPS, BLOCK_ANTENNAS))
        ratios = counts.astype(jnp.float32) / projected_counts

        def backward(args):
            tile_index, estimate, sens_tile = args
            coverage_value = tile_coverage(tile_index, clutter, antenna_settings, flattened_lists, flattened_counts)
            picked = ratios[flattened_lists[tile_index]]
            backsum = jnp.einsum('sta,sap->tp', picked, coverage_value, precision=highest)
            return estimate * backsum / sens_tile[None, :]

        est_tiles = lax.map(backward, (tile_ids, est_tiles, sensitivity))
    return est_tiles.reshape(N_ROW, N_COL, QUARTER_MAPS, TR, TC).transpose(2, 0, 3, 1, 4).reshape(QUARTER_MAPS, GR, GC)
```

```python
import functools
import jax
import jax.numpy as jnp
from jax import lax
from jax.experimental import pallas as pl
from jax.experimental.pallas import tpu as pltpu
from jax.sharding import PartitionSpec as P

ITERS = 2
LOG2E = 1.4426950408889634
CLUTTER_MAX = 1.5
STEP = 4
LO_SCALE = 65536.0
LO_TYPE = jnp.float8_e5m2
BIG = 1e38
f32 = jnp.float32
bf16 = jnp.bfloat16


def split(x):
    hi = x.astype(bf16)
    return hi, (x - hi.astype(f32)).astype(bf16)


def antenna_scale(record):
    return record[3:4, :] * jnp.exp2(jnp.maximum(record[4:5, :] * (-LOG2E * CLUTTER_MAX), 0.0))


def build_kernel(tab, origin, records, clut, est2, hi, lo, part, *, rows, cols):
    step = pl.program_id(0)
    maps = part.shape[1]
    for k in range(STEP):
        block = tab[step * STEP + k]
        lanes = pl.ds(k * 128, 128)

        @pl.when(block >= 0)
        def _():
            record = records[block]
            antenna_row = record[0:1, :]
            inv = 1.0 / (record[2:3, :] * record[2:3, :])
            slope = record[4:5, :] * (-LOG2E)
            peak = jnp.exp2(jnp.maximum(slope * CLUTTER_MAX, 0.0))
            inv = inv * peak
            column = (
                origin[1] + lax.broadcasted_iota(jnp.int32, (cols, 128), 0)
            ).astype(f32) + 0.5
            across = column - record[1:2, :]
            across = jnp.minimum(across * across * inv, BIG)
            slope8 = jnp.broadcast_to(slope, (8, 128))

            @pl.loop(0, rows)
            def _(r):
                down = (origin[0] + r).astype(f32) + 0.5 - antenna_row
                down = jnp.minimum(peak + down * down * inv, BIG)
                at = pl.multiple_of(r * cols, cols)
                power = jnp.exp2(clut[pl.ds(at, cols), :] * slope)
                den = across + down
                guess = pl.reciprocal(den, approx=True)
                guess = guess * (2.0 - den * guess)
                value = power * guess
                top = value.astype(bf16)
                hi[pl.ds(at, cols), lanes] = top
                lo[pl.ds(at, cols), lanes] = (
                    (value - top.astype(f32)) * LO_SCALE
                ).astype(LO_TYPE)

        @pl.when(block < 0)
        def _():
            hi[:, lanes] = jnp.zeros((rows * cols, 128), bf16)
            lo[:, lanes] = jnp.zeros((rows * cols, 128), LO_TYPE)

    forward_dot(tab, step, records, est2, hi, lo, part, maps)


def forward_dot(tab, step, records, est2, hi, lo, part, maps):
    both = jnp.dot(est2[...], hi[...], preferred_element_type=f32)
    low = jnp.dot(est2[:maps, :], lo[...].astype(bf16), preferred_element_type=f32)
    total = both[:maps, :] + (both[maps:, :] + low * (1.0 / LO_SCALE))
    for k in range(STEP):
        scale = antenna_scale(records[jnp.maximum(tab[step * STEP + k], 0)])
        part[k] = total[:, k * 128 : (k + 1) * 128] * scale


def forward_kernel(tab, records, est2, hi, lo, part):
    forward_dot(tab, pl.program_id(0), records, est2, hi, lo, part, part.shape[1])


def backward_kernel(tab, records, ratios, est, sens_in, hi, lo, est_out, *rest, first):
    if first:
        est2_out, sens_out, acc = rest
    else:
        (acc,) = rest
    step = pl.program_id(0)
    maps = est.shape[0]
    n_pixels = est.shape[1]

    @pl.when(step == 0)
    def _():
        acc[...] = jnp.zeros_like(acc)

    lhs = []
    low = []
    for k in range(STEP):
        block = tab[step * STEP + k]
        live = block >= 0
        scale = antenna_scale(records[jnp.maximum(block, 0)])
        ratio = jnp.where(live, ratios[k] * scale, 0.0)
        parts = [ratio]
        if first:
            ones = jnp.where(live, jnp.broadcast_to(scale, (16, 128)), 0.0)
            parts.append(ones)
        stack = jnp.concatenate(parts, axis=0)
        top, rest_of = split(stack)
        lhs.append(jnp.concatenate([top, rest_of], axis=0))
        low.append((top.astype(f32) * (1.0 / LO_SCALE)).astype(bf16))
    lhs = jnp.concatenate(lhs, axis=1)
    low = jnp.concatenate(low, axis=1)
    height = low.shape[0]
    chunk = 512
    dims = (((1,), (1,)), ((), ()))

    @pl.loop(0, n_pixels // chunk)
    def _(c):
        at = pl.multiple_of(c * chunk, chunk)
        wide = lax.dot_general(lhs, hi[pl.ds(at, chunk), :], dims, preferred_element_type=f32)
        thin = lax.dot_general(
            low, lo[pl.ds(at, chunk), :].astype(bf16), dims, preferred_element_type=f32
        )
        acc[:, pl.ds(at, chunk)] += wide[:height, :] + (wide[height:, :] + thin)

    @pl.when(step == pl.num_programs(0) - 1)
    def _():
        if first:
            sens = acc[maps : maps + 1, :]
            sens_out[...] = jnp.broadcast_to(sens, sens_out.shape)
        else:
            sens = sens_in[0:1, :]
        new = est[...] * acc[:maps, :] / sens
        est_out[...] = new
        if first:
            top, rest_of = split(new)
            est2_out[:maps, :] = top
            est2_out[maps:, :] = rest_of


def combine_kernel(tab, recv, out):
    out[...] = jnp.zeros_like(out)

    @pl.loop(0, recv.shape[0])
    def _(i):
        local = tab[i]

        @pl.when(local >= 0)
        def _():
            out[local] = out[local] + recv[i]


def pick_kernel(tab, table, out):
    @pl.loop(0, out.shape[0])
    def _(i):
        out[i] = table[jnp.maximum(tab[i], 0)]


def params(mib):
    return pltpu.CompilerParams(vmem_limit_bytes=mib << 20)


def spec(shape, index):
    return pl.BlockSpec(shape, index)


def whole(shape):
    return pl.BlockSpec(shape, lambda *_: (0,) * len(shape))


def build(tab, origin, records, clut, est2, rows, cols):
    slots = tab.shape[0]
    maps2, n_pixels = est2.shape
    maps = maps2 // 2
    wide = STEP * 128
    return pl.pallas_call(
        functools.partial(build_kernel, rows=rows, cols=cols),
        grid_spec=pltpu.PrefetchScalarGridSpec(
            num_scalar_prefetch=2,
            grid=(slots // STEP,),
            in_specs=[whole(records.shape), whole(clut.shape), whole(est2.shape)],
            out_specs=[
                spec((n_pixels, wide), lambda i, *_: (0, i)),
                spec((n_pixels, wide), lambda i, *_: (0, i)),
                spec((STEP, maps, 128), lambda i, *_: (i, 0, 0)),
            ],
        ),
        out_shape=[
            jax.ShapeDtypeStruct((n_pixels, slots * 128), bf16),
            jax.ShapeDtypeStruct((n_pixels, slots * 128), LO_TYPE),
            jax.ShapeDtypeStruct((slots, maps, 128), f32),
        ],
        compiler_params=params(56),
        name="build_cover",
    )(tab, origin, records, clut, est2)


def forward(tab, records, est2, hi, lo):
    slots = tab.shape[0]
    maps2, n_pixels = est2.shape
    maps = maps2 // 2
    wide = STEP * 128
    return pl.pallas_call(
        forward_kernel,
        grid_spec=pltpu.PrefetchScalarGridSpec(
            num_scalar_prefetch=1,
            grid=(slots // STEP,),
            in_specs=[
                whole(records.shape),
                whole(est2.shape),
                spec((n_pixels, wide), lambda i, *_: (0, i)),
                spec((n_pixels, wide), lambda i, *_: (0, i)),
            ],
            out_specs=spec((STEP, maps, 128), lambda i, *_: (i, 0, 0)),
        ),
        out_shape=jax.ShapeDtypeStruct((slots, maps, 128), f32),
        compiler_params=params(56),
        name="forward_product",
    )(tab, records, est2, hi, lo)


def backward(tab, records, ratios, est, sens, hi, lo, first):
    slots = tab.shape[0]
    maps, n_pixels = est.shape
    wide = STEP * 128
    out_specs = [whole((maps, n_pixels))]
    out_shape = [jax.ShapeDtypeStruct((maps, n_pixels), f32)]
    if first:
        out_specs += [whole((2 * maps, n_pixels)), whole((8, n_pixels))]
        out_shape += [
            jax.ShapeDtypeStruct((2 * maps, n_pixels), bf16),
            jax.ShapeDtypeStruct((8, n_pixels), f32),
        ]
    return pl.pallas_call(
        functools.partial(backward_kernel, first=first),
        grid_spec=pltpu.PrefetchScalarGridSpec(
            num_scalar_prefetch=1,
            grid=(slots // STEP,),
            in_specs=[
                whole(records.shape),
                spec((STEP, maps, 128), lambda i, *_: (i, 0, 0)),
                whole(est.shape),
                whole(sens.shape),
                spec((n_pixels, wide), lambda i, *_: (0, i)),
                spec((n_pixels, wide), lambda i, *_: (0, i)),
            ],
            out_specs=out_specs,
            scratch_shapes=[pltpu.VMEM((maps + (16 if first else 0), n_pixels), f32)],
        ),
        out_shape=out_shape,
        compiler_params=params(56),
        name="backward_product",
    )(tab, records, ratios, est, sens, hi, lo)


def combine(tab, recv, n_out):
    return pl.pallas_call(
        combine_kernel,
        grid_spec=pltpu.PrefetchScalarGridSpec(
            num_scalar_prefetch=1,
            grid=(1,),
            in_specs=[whole(recv.shape)],
            out_specs=whole((n_out,) + recv.shape[1:]),
        ),
        out_shape=jax.ShapeDtypeStruct((n_out,) + recv.shape[1:], f32),
        compiler_params=params(32),
        name="combine_slots",
    )(tab, recv)


def pick(tab, table):
    shape = (tab.shape[0],) + table.shape[1:]
    return pl.pallas_call(
        pick_kernel,
        grid_spec=pltpu.PrefetchScalarGridSpec(
            num_scalar_prefetch=1,
            grid=(1,),
            in_specs=[whole(table.shape)],
            out_specs=whole(shape),
        ),
        out_shape=jax.ShapeDtypeStruct(shape, f32),
        compiler_params=params(32),
        name="pick_slots",
    )(tab, table)


def slot_tables(lists, listed, n_groups, per_group):
    slots = lists.shape[1]
    index = jnp.arange(slots, dtype=jnp.int32)
    live = index[None, :] < listed[:, None]
    group = jnp.where(live, lists // per_group, -1)
    same = (group[:, :, None] == group[:, None, :]) & (index[None, None, :] < index[None, :, None])
    place = jnp.sum(same.astype(jnp.int32), axis=2)
    groups = jnp.arange(n_groups, dtype=jnp.int32)
    hit = (group[:, None, None, :] == groups[None, None, :, None]) & (
        place[:, None, None, :] == jnp.arange(2, dtype=jnp.int32)[None, :, None, None]
    )
    return jnp.sum(jnp.where(hit, lists[:, None, None, :] + 1, 0), axis=3) - 1


def shards(initial_estimate0, clutter, counts, antenna_settings, tile_block_list, tile_block_count):
    maps, rows, cols = initial_estimate0.shape
    n_pixels = rows * cols
    n_row = lax.axis_size("row")
    n_col = lax.axis_size("col")
    row = lax.axis_index("row")
    col = lax.axis_index("col")
    slots = tile_block_list.shape[2]

    record = jnp.zeros((8, 128), f32)
    record = lax.dynamic_update_slice(record, antenna_settings[0], (0, 0))
    meta = jnp.concatenate(
        [tile_block_list.reshape(slots), tile_block_count.reshape(1)]
    ).astype(f32)
    record = lax.dynamic_update_slice(record, meta[None, :], (5, 0))
    mine = lax.all_to_all(jnp.broadcast_to(record, (n_col, 8, 128)), "col", 0, 0, tiled=True)
    every = lax.all_to_all(
        jnp.broadcast_to(mine, (n_row, n_col, 8, 128)), "row", 0, 0, tiled=True
    )
    records = every.reshape(n_row * n_col, 8, 128)
    column_meta = lax.dynamic_index_in_dim(every[:, :, 5, :], col, 1, keepdims=False)
    column_meta = column_meta.astype(jnp.int32)
    tables = slot_tables(column_meta[:, :slots], column_meta[:, slots], n_row, n_col)
    tab = lax.dynamic_index_in_dim(tables, row, 0, keepdims=False).reshape(2 * n_row)
    theirs = lax.dynamic_index_in_dim(tables, row, 2, keepdims=False)
    theirs = jnp.where(theirs >= 0, theirs - row * n_col, -1).T.reshape(2 * n_row)

    origin = jnp.stack([row * rows, col * cols]).astype(jnp.int32)
    est = initial_estimate0.reshape(maps, n_pixels)
    clut = jnp.broadcast_to(clutter.reshape(n_pixels, 1), (n_pixels, 128))
    top = est.astype(bf16)
    est2 = jnp.concatenate([top, (est - top.astype(f32)).astype(bf16)], axis=0)
    sens = jnp.zeros((8, n_pixels), f32)
    wanted = counts[0].astype(f32)

    hi, lo, part = build(tab, origin, records, clut, est2, rows, cols)
    for sweep in range(ITERS):
        if sweep > 0:
            part = forward(tab, records, est2, hi, lo)
        part = part.reshape(2, n_row, maps, 128)
        recv = lax.all_to_all(part, "row", 1, 1, tiled=True)
        group_sum = combine(theirs, recv.reshape(2 * n_row, maps, 128), n_col)
        pieces = lax.all_to_all(group_sum, "col", 0, 0, tiled=True)
        ratio = wanted / jnp.sum(pieces, axis=0)
        table = lax.all_gather(ratio, "col", axis=0, tiled=False)
        sent = pick(theirs, table).reshape(2, n_row, maps, 128)
        back = lax.all_to_all(sent, "row", 1, 1, tiled=True).reshape(2 * n_row, maps, 128)
        if sweep == 0:
            est, est2, sens = backward(tab, records, back, est, sens, hi, lo, True)
        else:
            (est,) = backward(tab, records, back, est, sens, hi, lo, False)
    return est.reshape(maps, rows, cols)


def solution(mesh):
    in_specs = (
        P(None, "row", "col"),
        P("row", "col"),
        P(("row", "col"), None, None),
        P(("row", "col"), None, None),
        P("row", "col", None),
        P("row", "col"),
    )
    out_specs = P(None, "row", "col")
    return jax.shard_map(shards, mesh=mesh, in_specs=in_specs, out_specs=out_specs, check_vma=False)
```

```python
import functools
import jax
import jax.numpy as jnp
from jax import lax
from jax.experimental import pallas as pl
from jax.experimental.pallas import tpu as pltpu
from jax.sharding import PartitionSpec as P

ITERS = 2
LOG2E = 1.4426950408889634
CLUTTER_MAX = 1.5
STEP = 4
STORE = 65536.0
INV_MAX = 1e37
SENS_ROWS = 16
LO_TYPE = jnp.float8_e5m2
BIG = 1e38
f32 = jnp.float32
bf16 = jnp.bfloat16


def split(x):
    hi = x.astype(bf16)
    return hi, (x - hi.astype(f32)).astype(bf16)


def antenna_scale(record):
    peak = jnp.exp2(jnp.maximum(record[4:5, :] * (-LOG2E * CLUTTER_MAX), 0.0))
    return record[3:4, :] * (peak * (1.0 / STORE))


def any_live(tab, step):
    live = tab[step * STEP] >= 0
    for k in range(1, STEP):
        live = jnp.logical_or(live, tab[step * STEP + k] >= 0)
    return live


def build_kernel(tab, origin, records, clut, est, hi, lo, part, *rest, rows, cols, first):
    step = pl.program_id(0)
    maps = part.shape[1]
    if first:
        est2, across = rest

        @pl.when(step == 0)
        def _():
            top, remainder = split(est[...])
            est2[:maps, :] = top
            est2[maps:, :] = remainder
    else:
        (across,) = rest
        est2 = est

    @pl.when(any_live(tab, step))
    def _():
        for k in range(STEP):
            block = tab[step * STEP + k]
            live = block >= 0
            record = records[jnp.maximum(block, 0)]
            slope = jnp.where(live, record[4:5, :] * (-LOG2E), 0.0)
            peak = jnp.exp2(jnp.maximum(slope * CLUTTER_MAX, 0.0)) * (1.0 / STORE)
            inv = jnp.minimum(1.0 / (record[2:3, :] * record[2:3, :]), INV_MAX) * peak
            inv = jnp.where(live, inv, 0.0)
            peak = jnp.where(live, peak, jnp.inf)
            down = (
                origin[0] + lax.broadcasted_iota(jnp.int32, (rows, 128), 0)
            ).astype(f32) + (0.5 - record[0:1, :])
            down = peak + down * down * inv
            stack = [down, inv, record[1:2, :], slope, jnp.zeros((125 - rows, 128), f32)]
            turned = jnp.concatenate(stack, axis=0).T
            column = (
                origin[1] + lax.broadcasted_iota(jnp.int32, (1, cols), 1)
            ).astype(f32) + 0.5
            gap = column - turned[:, rows + 1 : rows + 2]
            across[k] = gap * gap * turned[:, rows : rows + 1]
            size = 32
            for a in range(0, 128, size):
                tilt = jnp.broadcast_to(turned[a : a + size, rows + 2 : rows + 3], (size, cols))
                side = across[k, a : a + size, :]
                at = slice(k * 128 + a, k * 128 + a + size)
                for r in range(rows):
                    den = side + turned[a : a + size, r : r + 1]
                    value = jnp.exp2(clut[r : r + 1, :] * tilt) / den
                    top = value.astype(bf16)
                    hi[at, r * cols : (r + 1) * cols] = top
                    lo[at, r * cols : (r + 1) * cols] = (value - top.astype(f32)).astype(LO_TYPE)
        forward_dot(tab, step, records, est2, hi, part, maps)


def forward_dot(tab, step, records, est2, hi, part, maps):
    both = lax.dot_general(
        est2[...], hi[...], (((1,), (1,)), ((), ())), preferred_element_type=f32
    )
    total = both[:maps, :] + both[maps:, :]
    for k in range(STEP):
        scale = antenna_scale(records[jnp.maximum(tab[step * STEP + k], 0)])
        part[k] = total[:, k * 128 : (k + 1) * 128] * scale


def forward_kernel(tab, records, est2, hi, part):
    step = pl.program_id(0)

    @pl.when(any_live(tab, step))
    def _():
        forward_dot(tab, step, records, est2, hi, part, part.shape[1])


def backward_kernel(tab, records, ratios, carry, est, hi, lo, *rest, start, last, sweep):
    step = pl.program_id(0)
    maps, n_pixels = est.shape
    if last and sweep == 0:
        est_out, est2_out, sens_out, acc = rest
    elif last:
        sens_in, est_out, acc = rest
    else:
        (acc,) = rest

    @pl.when(step == 0)
    def _():
        if start:
            acc[...] = jnp.zeros_like(acc)
        else:
            acc[...] = carry[...]

    @pl.when(any_live(tab, step))
    def _():
        wide = []
        thin = []
        for k in range(STEP):
            block = tab[step * STEP + k]
            live = block >= 0
            scale = antenna_scale(records[jnp.maximum(block, 0)])
            stack = jnp.where(live, ratios[k] * scale, 0.0)
            if sweep == 0:
                ones = jnp.where(live, jnp.broadcast_to(scale, (SENS_ROWS, 128)), 0.0)
                stack = jnp.concatenate([stack, ones], axis=0)
            top, remainder = split(stack)
            wide.append(jnp.concatenate([top, remainder], axis=0))
            thin.append(top)
        wide = jnp.concatenate(wide, axis=1)
        thin = jnp.concatenate(thin, axis=1)
        height = thin.shape[0]
        chunk = 512
        for at in range(0, n_pixels, chunk):
            both = jnp.dot(wide, hi[:, at : at + chunk], preferred_element_type=f32)
            low = jnp.dot(thin, lo[:, at : at + chunk], preferred_element_type=f32)
            acc[:, at : at + chunk] += both[:height, :] + (both[height:, :] + low)

    if last:

        @pl.when(step == pl.num_programs(0) - 1)
        def _():
            if sweep == 0:
                sens = acc[maps : maps + 1, :]
                sens_out[...] = jnp.broadcast_to(sens, sens_out.shape)
            else:
                sens = sens_in[0:1, :]
            new = est[...] * acc[:maps, :] / sens
            est_out[...] = new
            if sweep == 0:
                top, remainder = split(new)
                est2_out[:maps, :] = top
                est2_out[maps:, :] = remainder


def combine_kernel(tab, recv0, recv1, out):
    out[...] = jnp.zeros_like(out)
    half = recv0.shape[0]
    for j, recv in enumerate((recv0, recv1)):

        @pl.loop(0, half)
        def _(i):
            local = tab[j * half + i]

            @pl.when(local >= 0)
            def _():
                out[local] = out[local] + recv[i]


def pick_kernel(tab, table, out0, out1):
    half = out0.shape[0]

    @pl.loop(0, half)
    def _(i):
        out0[i] = table[jnp.maximum(tab[i], 0)]
        out1[i] = table[jnp.maximum(tab[half + i], 0)]


def params(mib):
    return pltpu.CompilerParams(vmem_limit_bytes=mib << 20)


def spec(shape, index):
    return pl.BlockSpec(shape, index)


def whole(shape):
    return pl.BlockSpec(shape, lambda *_: (0,) * len(shape))


def build(tab, origin, records, clut, est, maps, rows, cols, first):
    slots = tab.shape[0]
    n_pixels = rows * cols
    tall = STEP * 128
    out_specs = [
        spec((tall, n_pixels), lambda i, *_: (i, 0)),
        spec((tall, n_pixels), lambda i, *_: (i, 0)),
        spec((STEP, maps, 128), lambda i, *_: (i, 0, 0)),
    ]
    out_shape = [
        jax.ShapeDtypeStruct((slots * 128, n_pixels), bf16),
        jax.ShapeDtypeStruct((slots * 128, n_pixels), LO_TYPE),
        jax.ShapeDtypeStruct((slots, maps, 128), f32),
    ]
    if first:
        out_specs.append(whole((2 * maps, n_pixels)))
        out_shape.append(jax.ShapeDtypeStruct((2 * maps, n_pixels), bf16))
    return pl.pallas_call(
        functools.partial(build_kernel, rows=rows, cols=cols, first=first),
        grid_spec=pltpu.PrefetchScalarGridSpec(
            num_scalar_prefetch=2,
            grid=(slots // STEP,),
            in_specs=[whole(records.shape), whole(clut.shape), whole(est.shape)],
            out_specs=out_specs,
            scratch_shapes=[pltpu.VMEM((STEP, 128, cols), f32)],
        ),
        out_shape=out_shape,
        compiler_params=params(56),
        name="build_cover",
    )(tab, origin, records, clut, est)


def forward(tab, records, est2, hi):
    slots = tab.shape[0]
    maps2, n_pixels = est2.shape
    maps = maps2 // 2
    tall = STEP * 128
    return pl.pallas_call(
        forward_kernel,
        grid_spec=pltpu.PrefetchScalarGridSpec(
            num_scalar_prefetch=1,
            grid=(slots // STEP,),
            in_specs=[
                whole(records.shape),
                whole(est2.shape),
                spec((tall, n_pixels), lambda i, *_: (i, 0)),
            ],
            out_specs=spec((STEP, maps, 128), lambda i, *_: (i, 0, 0)),
        ),
        out_shape=jax.ShapeDtypeStruct((slots, maps, 128), f32),
        compiler_params=params(56),
        name="forward_product",
    )(tab, records, est2, hi)


def backward(tab, records, ratios, carry, est, hi, lo, sens, start, last, sweep):
    slots = tab.shape[0]
    maps, n_pixels = est.shape
    tall = STEP * 128
    height = maps + (SENS_ROWS if sweep == 0 else 0)
    if carry is None:
        carry = jnp.zeros((8, 128), f32)
    operands = [records, ratios, carry, est, hi, lo]
    in_specs = [
        whole(records.shape),
        spec((STEP, maps, 128), lambda i, *_: (i, 0, 0)),
        whole(carry.shape),
        whole(est.shape),
        spec((tall, n_pixels), lambda i, *_: (i, 0)),
        spec((tall, n_pixels), lambda i, *_: (i, 0)),
    ]
    scratch = [pltpu.VMEM((height, n_pixels), f32)]
    if not last:
        out_specs = [whole((height, n_pixels))]
        out_shape = [jax.ShapeDtypeStruct((height, n_pixels), f32)]
        scratch = []
    else:
        out_specs = [whole((maps, n_pixels))]
        out_shape = [jax.ShapeDtypeStruct((maps, n_pixels), f32)]
        if sweep == 0:
            out_specs += [whole((2 * maps, n_pixels)), whole((8, n_pixels))]
            out_shape += [
                jax.ShapeDtypeStruct((2 * maps, n_pixels), bf16),
                jax.ShapeDtypeStruct((8, n_pixels), f32),
            ]
        else:
            operands.append(sens)
            in_specs.append(whole(sens.shape))
    return pl.pallas_call(
        functools.partial(backward_kernel, start=start, last=last, sweep=sweep),
        grid_spec=pltpu.PrefetchScalarGridSpec(
            num_scalar_prefetch=1,
            grid=(slots // STEP,),
            in_specs=in_specs,
            out_specs=out_specs,
            scratch_shapes=scratch,
        ),
        out_shape=out_shape,
        compiler_params=params(56),
        name="backward_product",
    )(tab, *operands)


def combine(tab, recv0, recv1, n_out):
    return pl.pallas_call(
        combine_kernel,
        grid_spec=pltpu.PrefetchScalarGridSpec(
            num_scalar_prefetch=1,
            grid=(1,),
            in_specs=[whole(recv0.shape), whole(recv1.shape)],
            out_specs=whole((n_out,) + recv0.shape[1:]),
        ),
        out_shape=jax.ShapeDtypeStruct((n_out,) + recv0.shape[1:], f32),
        compiler_params=params(32),
        name="combine_slots",
    )(tab, recv0, recv1)


def pick(tab, table):
    shape = (tab.shape[0] // 2,) + table.shape[1:]
    return pl.pallas_call(
        pick_kernel,
        grid_spec=pltpu.PrefetchScalarGridSpec(
            num_scalar_prefetch=1,
            grid=(1,),
            in_specs=[whole(table.shape)],
            out_specs=[whole(shape), whole(shape)],
        ),
        out_shape=[jax.ShapeDtypeStruct(shape, f32)] * 2,
        compiler_params=params(32),
        name="pick_slots",
    )(tab, table)


def slot_tables(lists, listed, n_groups, per_group):
    slots = lists.shape[1]
    index = jnp.arange(slots, dtype=jnp.int32)
    live = index[None, :] < listed[:, None]
    group = jnp.where(live, lists // per_group, -1)
    same = (group[:, :, None] == group[:, None, :]) & (index[None, None, :] < index[None, :, None])
    place = jnp.sum(same.astype(jnp.int32), axis=2)
    groups = jnp.arange(n_groups, dtype=jnp.int32)
    hit = (group[:, None, None, :] == groups[None, None, :, None]) & (
        place[:, None, None, :] == jnp.arange(2, dtype=jnp.int32)[None, :, None, None]
    )
    return jnp.sum(jnp.where(hit, lists[:, None, None, :] + 1, 0), axis=3) - 1


def shards(initial_estimate0, clutter, counts, antenna_settings, tile_block_list, tile_block_count):
    maps, rows, cols = initial_estimate0.shape
    n_pixels = rows * cols
    n_row = lax.axis_size("row")
    n_col = lax.axis_size("col")
    row = lax.axis_index("row")
    col = lax.axis_index("col")
    slots = tile_block_list.shape[2]

    record = jnp.zeros((8, 128), f32)
    record = lax.dynamic_update_slice(record, antenna_settings[0], (0, 0))
    meta = jnp.concatenate(
        [tile_block_list.reshape(slots), tile_block_count.reshape(1)]
    ).astype(f32)
    record = lax.dynamic_update_slice(record, meta[None, :], (5, 0))
    mine = lax.all_to_all(jnp.broadcast_to(record, (n_col, 8, 128)), "col", 0, 0, tiled=True)
    every = lax.all_to_all(
        jnp.broadcast_to(mine, (n_row, n_col, 8, 128)), "row", 0, 0, tiled=True
    )
    records = every.reshape(n_row * n_col, 8, 128)
    column_meta = lax.dynamic_index_in_dim(every[:, :, 5, :], col, 1, keepdims=False)
    column_meta = column_meta.astype(jnp.int32)
    tables = slot_tables(column_meta[:, :slots], column_meta[:, slots], n_row, n_col)
    tab = lax.dynamic_index_in_dim(tables, row, 0, keepdims=False).reshape(2 * n_row)
    theirs = lax.dynamic_index_in_dim(tables, row, 2, keepdims=False)
    theirs = jnp.where(theirs >= 0, theirs - row * n_col, -1).T.reshape(2 * n_row)

    origin = jnp.stack([row * rows, col * cols]).astype(jnp.int32)
    est = initial_estimate0.reshape(maps, n_pixels)
    wanted = counts[0].astype(f32)
    tabs = (tab[:n_row], tab[n_row:])

    hi0, lo0, part0, est2 = build(
        tabs[0], origin, records, clutter, est, maps, rows, cols, True
    )
    recv0 = lax.all_to_all(part0, "row", 0, 0, tiled=True)
    hi1, lo1, part1 = build(tabs[1], origin, records, clutter, est2, maps, rows, cols, False)
    recv1 = lax.all_to_all(part1, "row", 0, 0, tiled=True)
    sens = None
    for sweep in range(ITERS):
        if sweep > 0:
            part0 = forward(tabs[0], records, est2, hi0)
            recv0 = lax.all_to_all(part0, "row", 0, 0, tiled=True)
            part1 = forward(tabs[1], records, est2, hi1)
            recv1 = lax.all_to_all(part1, "row", 0, 0, tiled=True)
        group_sum = combine(theirs, recv0, recv1, n_col)
        pieces = lax.all_to_all(group_sum, "col", 0, 0, tiled=True)
        ratio = wanted / jnp.sum(pieces, axis=0)
        table = lax.all_gather(ratio, "col", axis=0, tiled=False)
        sent0, sent1 = pick(theirs, table)
        back0 = lax.all_to_all(sent0, "row", 0, 0, tiled=True)
        back1 = lax.all_to_all(sent1, "row", 0, 0, tiled=True)
        (carry,) = backward(
            tabs[0], records, back0, None, est, hi0, lo0, sens, True, False, sweep
        )
        done = backward(
            tabs[1], records, back1, carry, est, hi1, lo1, sens, False, True, sweep
        )
        if sweep == 0:
            est, est2, sens = done
        else:
            (est,) = done
    return est.reshape(maps, rows, cols)


def solution(mesh):
    in_specs = (
        P(None, "row", "col"),
        P("row", "col"),
        P(("row", "col"), None, None),
        P(("row", "col"), None, None),
        P("row", "col", None),
        P("row", "col"),
    )
    out_specs = P(None, "row", "col")
    return jax.shard_map(shards, mesh=mesh, in_specs=in_specs, out_specs=out_specs, check_vma=False)
```

```python
import functools
import jax
import jax.numpy as jnp
from jax import lax
from jax.experimental import pallas as pl
from jax.experimental.pallas import tpu as pltpu
from jax.sharding import PartitionSpec as P

ITERS = 2
LOG2E = 1.4426950408889634
CLUTTER_MAX = 1.5
STEP = 4
STORE = 65536.0
INV_MAX = 1e37
SENS_ROWS = 16
LO_TYPE = jnp.float8_e5m2
BIG = 1e38
f32 = jnp.float32
bf16 = jnp.bfloat16


def split(x):
    hi = x.astype(bf16)
    return hi, (x - hi.astype(f32)).astype(bf16)


def wide_pair(x):
    top = lax.reduce_precision(x, 8, 7)
    pair = jnp.stack([top, x - top], axis=1)
    pair = jnp.pad(pair, ((0, 0), (0, 0), (0, 128 - x.shape[1])))
    return pair.reshape(x.shape[0], 256).astype(bf16)


def antenna_scale(record):
    peak = jnp.exp2(jnp.maximum(record[4:5, :] * (-LOG2E * CLUTTER_MAX), 0.0))
    return record[3:4, :] * (peak * (1.0 / STORE))


def any_live(tab, step):
    live = tab[step * STEP] >= 0
    for k in range(1, STEP):
        live = jnp.logical_or(live, tab[step * STEP + k] >= 0)
    return live


def build_kernel(tab, origin, records, clut, est2, *rest, rows, cols):
    hi, lo, part, across = rest[-4:]
    step = pl.program_id(0)
    maps = part.shape[1]

    @pl.when(any_live(tab, step))
    def _():
        for k in range(STEP):
            block = tab[step * STEP + k]
            live = block >= 0
            record = records[jnp.maximum(block, 0)]
            slope = jnp.where(live, record[4:5, :] * (-LOG2E), 0.0)
            peak = jnp.exp2(jnp.maximum(slope * CLUTTER_MAX, 0.0)) * (1.0 / STORE)
            inv = jnp.minimum(1.0 / (record[2:3, :] * record[2:3, :]), INV_MAX) * peak
            inv = jnp.where(live, inv, 0.0)
            peak = jnp.where(live, peak, jnp.inf)
            down = (
                origin[0] + lax.broadcasted_iota(jnp.int32, (rows, 128), 0)
            ).astype(f32) + (0.5 - record[0:1, :])
            down = peak + down * down * inv
            stack = [down, inv, record[1:2, :], slope, jnp.zeros((125 - rows, 128), f32)]
            turned = jnp.concatenate(stack, axis=0).T
            column = (
                origin[1] + lax.broadcasted_iota(jnp.int32, (1, cols), 1)
            ).astype(f32) + 0.5
            gap = column - turned[:, rows + 1 : rows + 2]
            across[k] = gap * gap * turned[:, rows : rows + 1]
            size = 32
            for a in range(0, 128, size):
                tilt = jnp.broadcast_to(turned[a : a + size, rows + 2 : rows + 3], (size, cols))
                side = across[k, a : a + size, :]
                at = slice(k * 128 + a, k * 128 + a + size)
                for r in range(rows):
                    den = side + turned[a : a + size, r : r + 1]
                    value = jnp.exp2(clut[r : r + 1, :] * tilt) / den
                    top = value.astype(bf16)
                    hi[at, r * cols : (r + 1) * cols] = top
                    lo[at, r * cols : (r + 1) * cols] = (value - top.astype(f32)).astype(LO_TYPE)
        forward_dot(tab, step, records, est2, hi, part, maps)


def forward_dot(tab, step, records, est2, hi, part, maps):
    both = jnp.dot(hi[...], est2[...], preferred_element_type=f32)
    total = both[:, :128] + both[:, 128:]
    for k in range(STEP):
        scale = antenna_scale(records[jnp.maximum(tab[step * STEP + k], 0)])
        part[k] = total[k * 128 : (k + 1) * 128, :].T[:maps, :] * scale


def forward_kernel(tab, records, est2, hi, part):
    step = pl.program_id(0)

    @pl.when(any_live(tab, step))
    def _():
        forward_dot(tab, step, records, est2, hi, part.at[:, 0], part.shape[2])


def backward_kernel(tab, records, ratios, est, hi, lo, *rest, sweep):
    step = pl.program_id(0)
    maps, n_pixels = est.shape
    if sweep == 0:
        est_out, est2_out, sens_out, acc = rest
    else:
        sens_in, est_out, acc = rest

    @pl.when(step == 0)
    def _():
        acc[...] = jnp.zeros_like(acc)

    @pl.when(any_live(tab, step))
    def _():
        wide = []
        thin = []
        for k in range(STEP):
            block = tab[step * STEP + k]
            live = block >= 0
            scale = antenna_scale(records[jnp.maximum(block, 0)])
            stack = jnp.where(live, ratios[k, 0] * scale, 0.0)
            if sweep == 0:
                ones = jnp.where(live, jnp.broadcast_to(scale, (SENS_ROWS, 128)), 0.0)
                stack = jnp.concatenate([stack, ones], axis=0)
            top, remainder = split(stack)
            wide.append(jnp.concatenate([top, remainder], axis=0))
            thin.append(top)
        wide = jnp.concatenate(wide, axis=1)
        thin = jnp.concatenate(thin, axis=1)
        height = thin.shape[0]
        chunk = 512
        for at in range(0, n_pixels, chunk):
            both = jnp.dot(wide, hi[:, at : at + chunk], preferred_element_type=f32)
            low = jnp.dot(thin, lo[:, at : at + chunk], preferred_element_type=f32)
            acc[:, at : at + chunk] += both[:height, :] + (both[height:, :] + low)

    @pl.when(step == pl.num_programs(0) - 1)
    def _():
        if sweep == 0:
            sens = acc[maps : maps + 1, :]
            sens_out[...] = jnp.broadcast_to(sens, sens_out.shape)
            new = est[...] * acc[:maps, :] / sens
            est_out[...] = new
            turned = jnp.concatenate([new, jnp.zeros((128 - maps, n_pixels), f32)], axis=0).T
            top, remainder = split(turned)
            est2_out[:, :128] = top
            est2_out[:, 128:] = remainder
        else:
            rows, cols = est_out.shape[1:]
            for r in range(rows):
                at = slice(r * cols, (r + 1) * cols)
                est_out[:, r, :] = est[:, at] * acc[:maps, at] / sens_in[0:1, at]


def combine_kernel(tab, *refs):
    out = refs[-1]
    recv = refs[:-1]
    groups = recv[0].shape[0]
    out[...] = jnp.zeros_like(out)
    for j in range(2):

        @pl.loop(0, groups)
        def _(i):
            local = tab[j * groups + i]

            @pl.when(local >= 0)
            def _():
                piece = recv[j][i] if len(recv) == 2 else recv[0][i, j]
                out[local] = out[local] + piece


def pick_kernel(tab, table, out):
    groups = out.shape[0]

    @pl.loop(0, groups)
    def _(i):
        for j in range(2):
            out[i, j] = table[jnp.maximum(tab[j * groups + i], 0)]


def params(mib):
    return pltpu.CompilerParams(vmem_limit_bytes=mib << 20)


def spec(shape, index):
    return pl.BlockSpec(shape, index)


def whole(shape):
    return pl.BlockSpec(shape, lambda *_: (0,) * len(shape))


def build(tab, origin, records, clut, est2, maps, rows, cols, half, stored):
    slots = tab.shape[0]
    n_pixels = rows * cols
    tall = STEP * 128
    steps = slots // STEP
    operands = [records, clut, est2]
    in_specs = [whole(x.shape) for x in operands]
    aliases = {}
    if half:
        operands += list(stored)
        in_specs += [pl.BlockSpec(memory_space=pl.ANY)] * 2
        aliases = {5: 0, 6: 1}
    return pl.pallas_call(
        functools.partial(build_kernel, rows=rows, cols=cols),
        grid_spec=pltpu.PrefetchScalarGridSpec(
            num_scalar_prefetch=2,
            grid=(steps,),
            in_specs=in_specs,
            out_specs=[
                spec((tall, n_pixels), lambda i, *_: (half * steps + i, 0)),
                spec((tall, n_pixels), lambda i, *_: (half * steps + i, 0)),
                spec((STEP, maps, 128), lambda i, *_: (i, 0, 0)),
            ],
            scratch_shapes=[pltpu.VMEM((STEP, 128, cols), f32)],
        ),
        out_shape=[
            jax.ShapeDtypeStruct((2 * slots * 128, n_pixels), bf16),
            jax.ShapeDtypeStruct((2 * slots * 128, n_pixels), LO_TYPE),
            jax.ShapeDtypeStruct((slots, maps, 128), f32),
        ],
        input_output_aliases=aliases,
        compiler_params=params(56),
        name="build_cover",
    )(tab, origin, *operands)


def place_spec(slots, maps):
    per = slots // 2 // STEP
    return spec((STEP, 1, maps, 128), lambda i, *_: (i % per, i // per, 0, 0))


def forward(tab, records, est2, hi, maps):
    slots = tab.shape[0]
    n_pixels = est2.shape[0]
    tall = STEP * 128
    return pl.pallas_call(
        forward_kernel,
        grid_spec=pltpu.PrefetchScalarGridSpec(
            num_scalar_prefetch=1,
            grid=(slots // STEP,),
            in_specs=[
                whole(records.shape),
                whole(est2.shape),
                spec((tall, n_pixels), lambda i, *_: (i, 0)),
            ],
            out_specs=place_spec(slots, maps),
        ),
        out_shape=jax.ShapeDtypeStruct((slots // 2, 2, maps, 128), f32),
        compiler_params=params(56),
        name="forward_product",
    )(tab, records, est2, hi)


def backward(tab, records, ratios, est, hi, lo, sens, sweep, rows, cols):
    slots = tab.shape[0]
    maps, n_pixels = est.shape
    tall = STEP * 128
    height = maps + (SENS_ROWS if sweep == 0 else 0)
    operands = [records, ratios, est, hi, lo]
    in_specs = [
        whole(records.shape),
        place_spec(slots, maps),
        whole(est.shape),
        spec((tall, n_pixels), lambda i, *_: (i, 0)),
        spec((tall, n_pixels), lambda i, *_: (i, 0)),
    ]
    if sweep == 0:
        shapes = [((maps, n_pixels), f32), ((n_pixels, 256), bf16), ((8, n_pixels), f32)]
    else:
        shapes = [((maps, rows, cols), f32)]
        operands.append(sens)
        in_specs.append(whole(sens.shape))
    return pl.pallas_call(
        functools.partial(backward_kernel, sweep=sweep),
        grid_spec=pltpu.PrefetchScalarGridSpec(
            num_scalar_prefetch=1,
            grid=(slots // STEP,),
            in_specs=in_specs,
            out_specs=[whole(shape) for shape, _ in shapes],
            scratch_shapes=[pltpu.VMEM((height, n_pixels), f32)],
        ),
        out_shape=[jax.ShapeDtypeStruct(shape, dtype) for shape, dtype in shapes],
        compiler_params=params(56),
        name="backward_product",
    )(tab, *operands)


def combine(tab, recv, n_out):
    shape = (n_out,) + recv[0].shape[-2:]
    return pl.pallas_call(
        combine_kernel,
        grid_spec=pltpu.PrefetchScalarGridSpec(
            num_scalar_prefetch=1,
            grid=(1,),
            in_specs=[whole(x.shape) for x in recv],
            out_specs=whole(shape),
        ),
        out_shape=jax.ShapeDtypeStruct(shape, f32),
        compiler_params=params(32),
        name="combine_slots",
    )(tab, *recv)


def pick(tab, table):
    shape = (tab.shape[0] // 2, 2) + table.shape[1:]
    return pl.pallas_call(
        pick_kernel,
        grid_spec=pltpu.PrefetchScalarGridSpec(
            num_scalar_prefetch=1,
            grid=(1,),
            in_specs=[whole(table.shape)],
            out_specs=whole(shape),
        ),
        out_shape=jax.ShapeDtypeStruct(shape, f32),
        compiler_params=params(32),
        name="pick_slots",
    )(tab, table)


def slot_tables(lists, listed, n_groups, per_group):
    slots = lists.shape[1]
    index = jnp.arange(slots, dtype=jnp.int32)
    live = index[None, :] < listed[:, None]
    group = jnp.where(live, lists // per_group, -1)
    same = (group[:, :, None] == group[:, None, :]) & (index[None, None, :] < index[None, :, None])
    place = jnp.sum(same.astype(jnp.int32), axis=2)
    groups = jnp.arange(n_groups, dtype=jnp.int32)
    hit = (group[:, None, None, :] == groups[None, None, :, None]) & (
        place[:, None, None, :] == jnp.arange(2, dtype=jnp.int32)[None, :, None, None]
    )
    return jnp.sum(jnp.where(hit, lists[:, None, None, :] + 1, 0), axis=3) - 1


def shards(initial_estimate0, clutter, counts, antenna_settings, tile_block_list, tile_block_count):
    maps, rows, cols = initial_estimate0.shape
    n_pixels = rows * cols
    n_row = lax.axis_size("row")
    n_col = lax.axis_size("col")
    row = lax.axis_index("row")
    col = lax.axis_index("col")
    slots = tile_block_list.shape[2]

    record = jnp.zeros((8, 128), f32)
    record = lax.dynamic_update_slice(record, antenna_settings[0], (0, 0))
    meta = jnp.concatenate(
        [tile_block_list.reshape(slots), tile_block_count.reshape(1)]
    ).astype(f32)
    record = lax.dynamic_update_slice(record, meta[None, :], (5, 0))
    mine = lax.all_to_all(jnp.broadcast_to(record, (n_col, 8, 128)), "col", 0, 0, tiled=True)
    every = lax.all_to_all(
        jnp.broadcast_to(mine, (n_row, n_col, 8, 128)), "row", 0, 0, tiled=True
    )
    records = every.reshape(n_row * n_col, 8, 128)
    own = slot_tables(
        tile_block_list.reshape(1, slots), tile_block_count.reshape(1), n_row, n_col
    )
    tab = own.reshape(2 * n_row)
    column_meta = lax.dynamic_index_in_dim(every[:, :, 5, :], col, 1, keepdims=False)
    column_meta = column_meta.astype(jnp.int32)
    tables = slot_tables(column_meta[:, :slots], column_meta[:, slots], n_row, n_col)
    theirs = lax.dynamic_index_in_dim(tables, row, 2, keepdims=False)
    theirs = jnp.where(theirs >= 0, theirs - row * n_col, -1).T.reshape(2 * n_row)

    origin = jnp.stack([row * rows, col * cols]).astype(jnp.int32)
    est = initial_estimate0.reshape(maps, n_pixels)
    est2 = wide_pair(initial_estimate0.transpose(1, 2, 0).reshape(n_pixels, maps))
    wanted = counts[0].astype(f32)
    tabs = (tab[:n_row], tab[n_row:])

    hi, lo, part = build(tabs[0], origin, records, clutter, est2, maps, rows, cols, 0, None)
    recv0 = lax.all_to_all(part, "row", 0, 0, tiled=True)
    hi, lo, part = build(tabs[1], origin, records, clutter, est2, maps, rows, cols, 1, (hi, lo))
    recv1 = lax.all_to_all(part, "row", 0, 0, tiled=True)
    recv = (recv0, recv1)
    sens = None
    for sweep in range(ITERS):
        if sweep > 0:
            part = forward(tab, records, est2, hi, maps)
            recv = (lax.all_to_all(part, "row", 0, 0, tiled=True),)
        group_sum = combine(theirs, recv, n_col)
        pieces = lax.all_to_all(group_sum, "col", 0, 0, tiled=True)
        ratio = wanted / jnp.sum(pieces, axis=0)
        table = lax.all_to_all(
            jnp.broadcast_to(ratio, (n_col,) + ratio.shape), "col", 0, 0, tiled=True
        )
        sent = pick(theirs, table)
        back = lax.all_to_all(sent, "row", 0, 0, tiled=True)
        done = backward(tab, records, back, est, hi, lo, sens, sweep, rows, cols)
        if sweep == 0:
            est, est2, sens = done
    return done[0]


def solution(mesh):
    in_specs = (
        P(None, "row", "col"),
        P("row", "col"),
        P(("row", "col"), None, None),
        P(("row", "col"), None, None),
        P("row", "col", None),
        P("row", "col"),
    )
    out_specs = P(None, "row", "col")
    return jax.shard_map(shards, mesh=mesh, in_specs=in_specs, out_specs=out_specs, check_vma=False)
```

```python
import functools
import jax
import jax.numpy as jnp
from jax import lax
from jax.experimental import pallas as pl
from jax.experimental.pallas import tpu as pltpu
from jax.sharding import PartitionSpec as P

ITERS = 2
LOG2E = 1.4426950408889634
CLUTTER_MAX = 1.5
STEP = 4
STORE = 65536.0
INV_MAX = 1e37
SENS_ROWS = 16
LO_TYPE = jnp.float8_e5m2
BIG = 1e38
f32 = jnp.float32
bf16 = jnp.bfloat16


def split(x):
    hi = x.astype(bf16)
    return hi, (x - hi.astype(f32)).astype(bf16)


def wide_pair(x):
    top = lax.reduce_precision(x, 8, 7)
    pair = jnp.stack([top, x - top], axis=1)
    pair = jnp.pad(pair, ((0, 0), (0, 0), (0, 128 - x.shape[1])))
    return pair.reshape(x.shape[0], 256).astype(bf16)


def antenna_scale(record):
    peak = jnp.exp2(jnp.maximum(record[4:5, :] * (-LOG2E * CLUTTER_MAX), 0.0))
    return record[3:4, :] * (peak * (1.0 / STORE))


def any_live(tab, step):
    live = tab[step * STEP] >= 0
    for k in range(1, STEP):
        live = jnp.logical_or(live, tab[step * STEP + k] >= 0)
    return live


def build_kernel(tab, origin, records, clut, est2, hi, lo, part, across, *, rows, cols):
    step = pl.program_id(0)

    @pl.when(any_live(tab, step))
    def _():
        for k in range(STEP):
            block = tab[step * STEP + k]
            live = block >= 0
            record = records[jnp.maximum(block, 0)]
            slope = jnp.where(live, record[4:5, :] * (-LOG2E), 0.0)
            peak = jnp.exp2(jnp.maximum(slope * CLUTTER_MAX, 0.0)) * (1.0 / STORE)
            inv = jnp.minimum(1.0 / (record[2:3, :] * record[2:3, :]), INV_MAX) * peak
            inv = jnp.where(live, inv, 0.0)
            peak = jnp.where(live, peak, jnp.inf)
            down = (
                origin[0] + lax.broadcasted_iota(jnp.int32, (rows, 128), 0)
            ).astype(f32) + (0.5 - record[0:1, :])
            down = peak + down * down * inv
            stack = [down, inv, record[1:2, :], slope, jnp.zeros((125 - rows, 128), f32)]
            turned = jnp.concatenate(stack, axis=0).T
            column = (
                origin[1] + lax.broadcasted_iota(jnp.int32, (1, cols), 1)
            ).astype(f32) + 0.5
            gap = column - turned[:, rows + 1 : rows + 2]
            across[k] = gap * gap * turned[:, rows : rows + 1]
            size = 32
            for a in range(0, 128, size):
                tilt = jnp.broadcast_to(turned[a : a + size, rows + 2 : rows + 3], (size, cols))
                side = across[k, a : a + size, :]
                at = slice(k * 128 + a, k * 128 + a + size)
                for r in range(rows):
                    den = side + turned[a : a + size, r : r + 1]
                    value = jnp.exp2(clut[r : r + 1, :] * tilt) / den
                    top = value.astype(bf16)
                    hi[at, r * cols : (r + 1) * cols] = top
                    lo[at, r * cols : (r + 1) * cols] = (value - top.astype(f32)).astype(LO_TYPE)
        forward_dot(tab, step, records, est2, hi, part)


def forward_dot(tab, step, records, est2, hi, part):
    maps = part.shape[2]
    both = jnp.dot(hi[...], est2[...], preferred_element_type=f32)
    total = both[:, :128] + both[:, 128:]
    for k in range(STEP):
        scale = antenna_scale(records[jnp.maximum(tab[step * STEP + k], 0)])
        part[k, 0] = total[k * 128 : (k + 1) * 128, :].T[:maps, :] * scale


def forward_kernel(tab, records, est2, hi, part):
    step = pl.program_id(0)

    @pl.when(any_live(tab, step))
    def _():
        forward_dot(tab, step, records, est2, hi, part)


def backward_kernel(tab, records, ratios, est, hi, lo, *rest, sweep):
    step = pl.program_id(0)
    maps, n_pixels = est.shape
    if sweep == 0:
        est_out, est2_out, sens_out, acc = rest
    else:
        sens_in, est_out, acc = rest

    @pl.when(step == 0)
    def _():
        acc[...] = jnp.zeros_like(acc)

    @pl.when(any_live(tab, step))
    def _():
        wide = []
        thin = []
        for k in range(STEP):
            block = tab[step * STEP + k]
            live = block >= 0
            scale = antenna_scale(records[jnp.maximum(block, 0)])
            stack = jnp.where(live, ratios[k, 0] * scale, 0.0)
            if sweep == 0:
                ones = jnp.where(live, jnp.broadcast_to(scale, (SENS_ROWS, 128)), 0.0)
                stack = jnp.concatenate([stack, ones], axis=0)
            top, remainder = split(stack)
            wide.append(jnp.concatenate([top, remainder], axis=0))
            thin.append(top)
        wide = jnp.concatenate(wide, axis=1)
        thin = jnp.concatenate(thin, axis=1)
        height = thin.shape[0]
        chunk = 512
        for at in range(0, n_pixels, chunk):
            both = jnp.dot(wide, hi[:, at : at + chunk], preferred_element_type=f32)
            low = jnp.dot(thin, lo[:, at : at + chunk], preferred_element_type=f32)
            acc[:, at : at + chunk] += both[:height, :] + (both[height:, :] + low)

    @pl.when(step == pl.num_programs(0) - 1)
    def _():
        if sweep == 0:
            sens = acc[maps : maps + 1, :]
            sens_out[...] = jnp.broadcast_to(sens, sens_out.shape)
            new = est[...] * acc[:maps, :] / sens
            est_out[...] = new
            turned = jnp.concatenate([new, jnp.zeros((128 - maps, n_pixels), f32)], axis=0).T
            top, remainder = split(turned)
            est2_out[:, :128] = top
            est2_out[:, 128:] = remainder
        else:
            rows, cols = est_out.shape[1:]
            for r in range(rows):
                at = slice(r * cols, (r + 1) * cols)
                est_out[:, r, :] = est[:, at] * acc[:maps, at] / sens_in[0:1, at]


def combine_kernel(tab, recv, out):
    groups = recv.shape[0]
    out[...] = jnp.zeros_like(out)

    @pl.loop(0, groups)
    def _(i):
        for j in range(2):
            local = tab[j * groups + i]

            @pl.when(local >= 0)
            def _():
                out[local] = out[local] + recv[i, j]


def pick_kernel(tab, table, out):
    groups = out.shape[0]

    @pl.loop(0, groups)
    def _(i):
        for j in range(2):
            out[i, j] = table[jnp.maximum(tab[j * groups + i], 0)]


def params(mib):
    return pltpu.CompilerParams(vmem_limit_bytes=mib << 20)


def spec(shape, index):
    return pl.BlockSpec(shape, index)


def whole(shape):
    return pl.BlockSpec(shape, lambda *_: (0,) * len(shape))


def place_spec(slots, maps):
    per = slots // 2 // STEP
    return spec((STEP, 1, maps, 128), lambda i, *_: (i % per, i // per, 0, 0))


def build(tab, origin, records, clut, est2, maps, rows, cols):
    slots = tab.shape[0]
    n_pixels = rows * cols
    tall = STEP * 128
    return pl.pallas_call(
        functools.partial(build_kernel, rows=rows, cols=cols),
        grid_spec=pltpu.PrefetchScalarGridSpec(
            num_scalar_prefetch=2,
            grid=(slots // STEP,),
            in_specs=[whole(records.shape), whole(clut.shape), whole(est2.shape)],
            out_specs=[
                spec((tall, n_pixels), lambda i, *_: (i, 0)),
                spec((tall, n_pixels), lambda i, *_: (i, 0)),
                place_spec(slots, maps),
            ],
            scratch_shapes=[pltpu.VMEM((STEP, 128, cols), f32)],
        ),
        out_shape=[
            jax.ShapeDtypeStruct((slots * 128, n_pixels), bf16),
            jax.ShapeDtypeStruct((slots * 128, n_pixels), LO_TYPE),
            jax.ShapeDtypeStruct((slots // 2, 2, maps, 128), f32),
        ],
        compiler_params=params(56),
        name="build_cover",
    )(tab, origin, records, clut, est2)


def forward(tab, records, est2, hi, maps):
    slots = tab.shape[0]
    n_pixels = est2.shape[0]
    tall = STEP * 128
    return pl.pallas_call(
        forward_kernel,
        grid_spec=pltpu.PrefetchScalarGridSpec(
            num_scalar_prefetch=1,
            grid=(slots // STEP,),
            in_specs=[
                whole(records.shape),
                whole(est2.shape),
                spec((tall, n_pixels), lambda i, *_: (i, 0)),
            ],
            out_specs=place_spec(slots, maps),
        ),
        out_shape=jax.ShapeDtypeStruct((slots // 2, 2, maps, 128), f32),
        compiler_params=params(56),
        name="forward_product",
    )(tab, records, est2, hi)


def backward(tab, records, ratios, est, hi, lo, sens, sweep, rows, cols):
    slots = tab.shape[0]
    maps, n_pixels = est.shape
    tall = STEP * 128
    height = maps + (SENS_ROWS if sweep == 0 else 0)
    operands = [records, ratios, est, hi, lo]
    in_specs = [
        whole(records.shape),
        place_spec(slots, maps),
        whole(est.shape),
        spec((tall, n_pixels), lambda i, *_: (i, 0)),
        spec((tall, n_pixels), lambda i, *_: (i, 0)),
    ]
    if sweep == 0:
        shapes = [((maps, n_pixels), f32), ((n_pixels, 256), bf16), ((8, n_pixels), f32)]
    else:
        shapes = [((maps, rows, cols), f32)]
        operands.append(sens)
        in_specs.append(whole(sens.shape))
    return pl.pallas_call(
        functools.partial(backward_kernel, sweep=sweep),
        grid_spec=pltpu.PrefetchScalarGridSpec(
            num_scalar_prefetch=1,
            grid=(slots // STEP,),
            in_specs=in_specs,
            out_specs=[whole(shape) for shape, _ in shapes],
            scratch_shapes=[pltpu.VMEM((height, n_pixels), f32)],
        ),
        out_shape=[jax.ShapeDtypeStruct(shape, dtype) for shape, dtype in shapes],
        compiler_params=params(56),
        name="backward_product",
    )(tab, *operands)


def combine(tab, recv, n_out):
    shape = (n_out,) + recv.shape[2:]
    return pl.pallas_call(
        combine_kernel,
        grid_spec=pltpu.PrefetchScalarGridSpec(
            num_scalar_prefetch=1,
            grid=(1,),
            in_specs=[whole(recv.shape)],
            out_specs=whole(shape),
        ),
        out_shape=jax.ShapeDtypeStruct(shape, f32),
        compiler_params=params(32),
        name="combine_slots",
    )(tab, recv)


def pick(tab, table):
    shape = (tab.shape[0] // 2, 2) + table.shape[1:]
    return pl.pallas_call(
        pick_kernel,
        grid_spec=pltpu.PrefetchScalarGridSpec(
            num_scalar_prefetch=1,
            grid=(1,),
            in_specs=[whole(table.shape)],
            out_specs=whole(shape),
        ),
        out_shape=jax.ShapeDtypeStruct(shape, f32),
        compiler_params=params(32),
        name="pick_slots",
    )(tab, table)


def slot_tables(lists, listed, n_groups, per_group):
    slots = lists.shape[1]
    index = jnp.arange(slots, dtype=jnp.int32)
    live = index[None, :] < listed[:, None]
    group = jnp.where(live, lists // per_group, -1)
    same = (group[:, :, None] == group[:, None, :]) & (index[None, None, :] < index[None, :, None])
    place = jnp.sum(same.astype(jnp.int32), axis=2)
    groups = jnp.arange(n_groups, dtype=jnp.int32)
    hit = (group[:, None, None, :] == groups[None, None, :, None]) & (
        place[:, None, None, :] == jnp.arange(2, dtype=jnp.int32)[None, :, None, None]
    )
    return jnp.sum(jnp.where(hit, lists[:, None, None, :] + 1, 0), axis=3) - 1


def exchange(x, both_places):
    def first(x):
        got = lax.all_to_all(x[:, 0], "row", 0, 0, tiled=True)
        return jnp.stack([got, jnp.zeros_like(got)], axis=1)

    def full(x):
        return lax.all_to_all(x, "row", 0, 0, tiled=True)

    return lax.cond(both_places, full, first, x)


def shards(initial_estimate0, clutter, counts, antenna_settings, tile_block_list, tile_block_count):
    maps, rows, cols = initial_estimate0.shape
    n_pixels = rows * cols
    n_row = lax.axis_size("row")
    n_col = lax.axis_size("col")
    row = lax.axis_index("row")
    col = lax.axis_index("col")
    slots = tile_block_list.shape[2]

    record = jnp.zeros((8, 128), f32)
    record = lax.dynamic_update_slice(record, antenna_settings[0], (0, 0))
    meta = jnp.concatenate(
        [tile_block_list.reshape(slots), tile_block_count.reshape(1)]
    ).astype(f32)
    record = lax.dynamic_update_slice(record, meta[None, :], (5, 0))
    mine = lax.all_to_all(jnp.broadcast_to(record, (n_col, 8, 128)), "col", 0, 0, tiled=True)
    every = lax.all_to_all(
        jnp.broadcast_to(mine, (n_row, n_col, 8, 128)), "row", 0, 0, tiled=True
    )
    records = every.reshape(n_row * n_col, 8, 128)
    own = slot_tables(
        tile_block_list.reshape(1, slots), tile_block_count.reshape(1), n_row, n_col
    )
    tab = own.reshape(2 * n_row)
    column_meta = lax.dynamic_index_in_dim(every[:, :, 5, :], col, 1, keepdims=False)
    column_meta = column_meta.astype(jnp.int32)
    tables = slot_tables(column_meta[:, :slots], column_meta[:, slots], n_row, n_col)
    theirs = lax.dynamic_index_in_dim(tables, row, 2, keepdims=False)
    theirs = jnp.where(theirs >= 0, theirs - row * n_col, -1).T.reshape(2 * n_row)

    both_places = jnp.any(tables[:, 1] >= 0)
    origin = jnp.stack([row * rows, col * cols]).astype(jnp.int32)
    est = initial_estimate0.reshape(maps, n_pixels)
    est2 = wide_pair(initial_estimate0.transpose(1, 2, 0).reshape(n_pixels, maps))
    wanted = counts[0].astype(f32)

    hi, lo, part = build(tab, origin, records, clutter, est2, maps, rows, cols)
    sens = None
    for sweep in range(ITERS):
        if sweep > 0:
            part = forward(tab, records, est2, hi, maps)
        group_sum = combine(theirs, exchange(part, both_places), n_col)
        pieces = lax.all_to_all(group_sum, "col", 0, 0, tiled=True)
        ratio = wanted / jnp.sum(pieces, axis=0)
        table = lax.all_to_all(
            jnp.broadcast_to(ratio, (n_col,) + ratio.shape), "col", 0, 0, tiled=True
        )
        sent = pick(theirs, table)
        back = exchange(sent, both_places)
        done = backward(tab, records, back, est, hi, lo, sens, sweep, rows, cols)
        if sweep == 0:
            est, est2, sens = done
    return done[0]


def solution(mesh):
    in_specs = (
        P(None, "row", "col"),
        P("row", "col"),
        P(("row", "col"), None, None),
        P(("row", "col"), None, None),
        P("row", "col", None),
        P("row", "col"),
    )
    out_specs = P(None, "row", "col")
    return jax.shard_map(shards, mesh=mesh, in_specs=in_specs, out_specs=out_specs, check_vma=False)
```

```python
import functools
import jax
import jax.numpy as jnp
from jax import lax
from jax.experimental import pallas as pl
from jax.experimental.pallas import tpu as pltpu
from jax.sharding import PartitionSpec as P

ITERS = 2
LOG2E = 1.4426950408889634
CLUTTER_MAX = 1.5
BUILD_STEP = 4
FORWARD_STEP = 8
BACK_STEP = 8
CHUNK = 512
STORE = 65536.0
INV_MAX = 1e37
SENS_ROWS = 16
LO_TYPE = jnp.float8_e5m2
BIG = 1e38
f32 = jnp.float32
bf16 = jnp.bfloat16


def split(x):
    hi = x.astype(bf16)
    return hi, (x - hi.astype(f32)).astype(bf16)


def wide_pair(x):
    top = lax.reduce_precision(x, 8, 7)
    pair = jnp.stack([top, x - top], axis=1)
    pair = jnp.pad(pair, ((0, 0), (0, 0), (0, 128 - x.shape[1])))
    return pair.reshape(x.shape[0], 256).astype(bf16)


def antenna_scale(record):
    peak = jnp.exp2(jnp.maximum(record[4:5, :] * (-LOG2E * CLUTTER_MAX), 0.0))
    return record[3:4, :] * (peak * (1.0 / STORE))


def any_live(tab, first, count):
    live = tab[first] >= 0
    for k in range(1, count):
        live = jnp.logical_or(live, tab[first + k] >= 0)
    return live


def build_kernel(tab, origin, records, clut, est2, hi, lo, part, across, *, rows, cols):
    step = pl.program_id(0)

    live_step = any_live(tab, step * BUILD_STEP // BACK_STEP * BACK_STEP, BACK_STEP)

    @pl.when(live_step)
    def _():
        for k in range(BUILD_STEP):
            block = tab[step * BUILD_STEP + k]
            live = block >= 0
            record = records[jnp.maximum(block, 0)]
            slope = jnp.where(live, record[4:5, :] * (-LOG2E), 0.0)
            peak = jnp.exp2(jnp.maximum(slope * CLUTTER_MAX, 0.0)) * (1.0 / STORE)
            inv = jnp.minimum(1.0 / (record[2:3, :] * record[2:3, :]), INV_MAX) * peak
            inv = jnp.where(live, inv, 0.0)
            peak = jnp.where(live, peak, jnp.inf)
            down = (
                origin[0] + lax.broadcasted_iota(jnp.int32, (rows, 128), 0)
            ).astype(f32) + (0.5 - record[0:1, :])
            down = peak + down * down * inv
            stack = [down, inv, record[1:2, :], slope, jnp.zeros((125 - rows, 128), f32)]
            turned = jnp.concatenate(stack, axis=0).T
            column = (
                origin[1] + lax.broadcasted_iota(jnp.int32, (1, cols), 1)
            ).astype(f32) + 0.5
            gap = column - turned[:, rows + 1 : rows + 2]
            across[k] = gap * gap * turned[:, rows : rows + 1]
            size = 32
            for a in range(0, 128, size):
                tilt = jnp.broadcast_to(turned[a : a + size, rows + 2 : rows + 3], (size, cols))
                side = across[k, a : a + size, :]
                at = slice(k * 128 + a, k * 128 + a + size)
                for r in range(rows):
                    den = side + turned[a : a + size, r : r + 1]
                    value = jnp.exp2(clut[r : r + 1, :] * tilt) / den
                    top = value.astype(bf16)
                    hi[at, r * cols : (r + 1) * cols] = top
                    lo[at, r * cols : (r + 1) * cols] = (value - top.astype(f32)).astype(LO_TYPE)
        forward_dot(tab, step, records, est2, hi, part)


def forward_dot(tab, step, records, est2, hi, part):
    count, _, maps, _ = part.shape
    both = jnp.dot(hi[...], est2[...], preferred_element_type=f32)
    total = both[:, :128] + both[:, 128:]
    for k in range(count):
        scale = antenna_scale(records[jnp.maximum(tab[step * count + k], 0)])
        part[k, 0] = total[k * 128 : (k + 1) * 128, :].T[:maps, :] * scale


def forward_kernel(tab, records, est2, hi, part):
    step = pl.program_id(0)
    count = part.shape[0]

    @pl.when(any_live(tab, step * count, count))
    def _():
        forward_dot(tab, step, records, est2, hi, part)


def backward_kernel(tab, records, ratios, est, hi, lo, *rest, sweep):
    step = pl.program_id(0)
    maps, n_pixels = est.shape
    if sweep == 0:
        est_out, est2_out, sens_out, acc = rest
    else:
        sens_in, est_out, acc = rest

    @pl.when(step == 0)
    def _():
        acc[...] = jnp.zeros_like(acc)

    @pl.when(any_live(tab, step * BACK_STEP, BACK_STEP))
    def _():
        wide = []
        thin = []
        for k in range(BACK_STEP):
            block = tab[step * BACK_STEP + k]
            live = block >= 0
            scale = antenna_scale(records[jnp.maximum(block, 0)])
            stack = jnp.where(live, ratios[k, 0] * scale, 0.0)
            if sweep == 0:
                ones = jnp.where(live, jnp.broadcast_to(scale, (SENS_ROWS, 128)), 0.0)
                stack = jnp.concatenate([stack, ones], axis=0)
            top, remainder = split(stack)
            wide.append(jnp.concatenate([top, remainder], axis=0))
            thin.append(top)
        wide = jnp.concatenate(wide, axis=1)
        thin = jnp.concatenate(thin, axis=1)
        height = thin.shape[0]
        chunk = CHUNK
        for at in range(0, n_pixels, chunk):
            both = jnp.dot(wide, hi[:, at : at + chunk], preferred_element_type=f32)
            low = jnp.dot(thin, lo[:, at : at + chunk], preferred_element_type=f32)
            acc[:, at : at + chunk] += both[:height, :] + (both[height:, :] + low)

    @pl.when(step == pl.num_programs(0) - 1)
    def _():
        if sweep == 0:
            sens = acc[maps : maps + 1, :]
            sens_out[...] = jnp.broadcast_to(sens, sens_out.shape)
            new = est[...] * acc[:maps, :] / sens
            est_out[...] = new
            turned = jnp.concatenate([new, jnp.zeros((128 - maps, n_pixels), f32)], axis=0).T
            top, remainder = split(turned)
            est2_out[:, :128] = top
            est2_out[:, 128:] = remainder
        else:
            rows, cols = est_out.shape[1:]
            for r in range(rows):
                at = slice(r * cols, (r + 1) * cols)
                est_out[:, r, :] = est[:, at] * acc[:maps, at] / sens_in[0:1, at]


def combine_kernel(tab, recv, out):
    groups = recv.shape[0]
    out[...] = jnp.zeros_like(out)

    @pl.loop(0, groups)
    def _(i):
        for j in range(2):
            local = tab[j * groups + i]

            @pl.when(local >= 0)
            def _():
                out[local] = out[local] + recv[i, j]


def pick_kernel(tab, table, out):
    groups = out.shape[0]

    @pl.loop(0, groups)
    def _(i):
        for j in range(2):
            out[i, j] = table[jnp.maximum(tab[j * groups + i], 0)]


def params(mib):
    return pltpu.CompilerParams(vmem_limit_bytes=mib << 20)


def spec(shape, index):
    return pl.BlockSpec(shape, index)


def whole(shape):
    return pl.BlockSpec(shape, lambda *_: (0,) * len(shape))


def place_spec(slots, maps, step):
    per = slots // 2 // step
    return spec((step, 1, maps, 128), lambda i, *_: (i % per, i // per, 0, 0))


def build(tab, origin, records, clut, est2, maps, rows, cols):
    slots = tab.shape[0]
    n_pixels = rows * cols
    tall = BUILD_STEP * 128
    return pl.pallas_call(
        functools.partial(build_kernel, rows=rows, cols=cols),
        grid_spec=pltpu.PrefetchScalarGridSpec(
            num_scalar_prefetch=2,
            grid=(slots // BUILD_STEP,),
            in_specs=[whole(records.shape), whole(clut.shape), whole(est2.shape)],
            out_specs=[
                spec((tall, n_pixels), lambda i, *_: (i, 0)),
                spec((tall, n_pixels), lambda i, *_: (i, 0)),
                place_spec(slots, maps, BUILD_STEP),
            ],
            scratch_shapes=[pltpu.VMEM((BUILD_STEP, 128, cols), f32)],
        ),
        out_shape=[
            jax.ShapeDtypeStruct((slots * 128, n_pixels), bf16),
            jax.ShapeDtypeStruct((slots * 128, n_pixels), LO_TYPE),
            jax.ShapeDtypeStruct((slots // 2, 2, maps, 128), f32),
        ],
        compiler_params=params(56),
        name="build_cover",
    )(tab, origin, records, clut, est2)


def forward(tab, records, est2, hi, maps):
    slots = tab.shape[0]
    n_pixels = est2.shape[0]
    tall = FORWARD_STEP * 128
    return pl.pallas_call(
        forward_kernel,
        grid_spec=pltpu.PrefetchScalarGridSpec(
            num_scalar_prefetch=1,
            grid=(slots // FORWARD_STEP,),
            in_specs=[
                whole(records.shape),
                whole(est2.shape),
                spec((tall, n_pixels), lambda i, *_: (i, 0)),
            ],
            out_specs=place_spec(slots, maps, FORWARD_STEP),
        ),
        out_shape=jax.ShapeDtypeStruct((slots // 2, 2, maps, 128), f32),
        compiler_params=params(56),
        name="forward_product",
    )(tab, records, est2, hi)


def backward(tab, records, ratios, est, hi, lo, sens, sweep, rows, cols):
    slots = tab.shape[0]
    maps, n_pixels = est.shape
    tall = BACK_STEP * 128
    height = maps + (SENS_ROWS if sweep == 0 else 0)
    operands = [records, ratios, est, hi, lo]
    in_specs = [
        whole(records.shape),
        place_spec(slots, maps, BACK_STEP),
        whole(est.shape),
        spec((tall, n_pixels), lambda i, *_: (i, 0)),
        spec((tall, n_pixels), lambda i, *_: (i, 0)),
    ]
    if sweep == 0:
        shapes = [((maps, n_pixels), f32), ((n_pixels, 256), bf16), ((8, n_pixels), f32)]
    else:
        shapes = [((maps, rows, cols), f32)]
        operands.append(sens)
        in_specs.append(whole(sens.shape))
    return pl.pallas_call(
        functools.partial(backward_kernel, sweep=sweep),
        grid_spec=pltpu.PrefetchScalarGridSpec(
            num_scalar_prefetch=1,
            grid=(slots // BACK_STEP,),
            in_specs=in_specs,
            out_specs=[whole(shape) for shape, _ in shapes],
            scratch_shapes=[pltpu.VMEM((height, n_pixels), f32)],
        ),
        out_shape=[jax.ShapeDtypeStruct(shape, dtype) for shape, dtype in shapes],
        compiler_params=params(56),
        name="backward_product",
    )(tab, *operands)


def combine(tab, recv, n_out):
    shape = (n_out,) + recv.shape[2:]
    return pl.pallas_call(
        combine_kernel,
        grid_spec=pltpu.PrefetchScalarGridSpec(
            num_scalar_prefetch=1,
            grid=(1,),
            in_specs=[whole(recv.shape)],
            out_specs=whole(shape),
        ),
        out_shape=jax.ShapeDtypeStruct(shape, f32),
        compiler_params=params(32),
        name="combine_slots",
    )(tab, recv)


def pick(tab, table):
    shape = (tab.shape[0] // 2, 2) + table.shape[1:]
    return pl.pallas_call(
        pick_kernel,
        grid_spec=pltpu.PrefetchScalarGridSpec(
            num_scalar_prefetch=1,
            grid=(1,),
            in_specs=[whole(table.shape)],
            out_specs=whole(shape),
        ),
        out_shape=jax.ShapeDtypeStruct(shape, f32),
        compiler_params=params(32),
        name="pick_slots",
    )(tab, table)


def slot_table(blocks, listed, n_groups, per_group):
    index = jnp.arange(blocks.shape[0], dtype=jnp.int32)
    group = jnp.where(index < listed, blocks // per_group, -1)
    same = (group[:, None] == group[None, :]) & (index[None, :] < index[:, None])
    place = jnp.sum(same.astype(jnp.int32), axis=1)
    key = jnp.where(group >= 0, place * n_groups + group, -1)
    hit = key[None, :] == jnp.arange(2 * n_groups, dtype=jnp.int32)[:, None]
    return jnp.sum(jnp.where(hit, blocks[None, :] + 1, 0), axis=1) - 1


def exchange(x, both_places):
    def first(x):
        got = lax.all_to_all(x[:, 0], "row", 0, 0, tiled=True)
        return jnp.stack([got, jnp.zeros_like(got)], axis=1)

    def full(x):
        return lax.all_to_all(x, "row", 0, 0, tiled=True)

    return lax.cond(both_places, full, first, x)


def shards(initial_estimate0, clutter, counts, antenna_settings, tile_block_list, tile_block_count):
    maps, rows, cols = initial_estimate0.shape
    n_pixels = rows * cols
    n_row = lax.axis_size("row")
    n_col = lax.axis_size("col")
    row = lax.axis_index("row")
    col = lax.axis_index("col")
    slots = tile_block_list.shape[2]

    record = jnp.pad(antenna_settings[0], ((0, 3), (0, 0)))
    mine = lax.all_to_all(jnp.broadcast_to(record, (n_col, 8, 128)), "col", 0, 0, tiled=True)
    tab = slot_table(tile_block_list.reshape(slots), tile_block_count.reshape(()), n_row, n_col)
    line = jnp.pad(tab.astype(f32), (0, 128 - 2 * n_row))
    mine, initial_estimate0 = lax.optimization_barrier((mine, initial_estimate0))
    here = lax.broadcasted_iota(jnp.int32, mine.shape, 1) == 5
    every = lax.all_to_all(
        jnp.broadcast_to(jnp.where(here, line, mine), (n_row, n_col, 8, 128)),
        "row",
        0,
        0,
        tiled=True,
    )
    records = every.reshape(n_row * n_col, 8, 128)
    tables = lax.dynamic_index_in_dim(every[:, :, 5, : 2 * n_row], col, 1, keepdims=False)
    tables = tables.astype(jnp.int32).reshape(n_row, 2, n_row)
    theirs = lax.dynamic_index_in_dim(tables, row, 2, keepdims=False)
    theirs = jnp.where(theirs >= 0, theirs - row * n_col, -1).T.reshape(2 * n_row)

    both_places = jnp.any(tables[:, 1] >= 0)
    origin = jnp.stack([row * rows, col * cols]).astype(jnp.int32)
    est = initial_estimate0.reshape(maps, n_pixels)
    est2 = wide_pair(initial_estimate0.transpose(1, 2, 0).reshape(n_pixels, maps))
    wanted = counts[0].astype(f32)

    hi, lo, part = build(tab, origin, records, clutter, est2, maps, rows, cols)
    sens = None
    for sweep in range(ITERS):
        if sweep > 0:
            part = forward(tab, records, est2, hi, maps)
        group_sum = combine(theirs, exchange(part, both_places), n_col)
        pieces = lax.all_to_all(group_sum, "col", 0, 0, tiled=True)
        ratio = wanted / jnp.sum(pieces, axis=0)
        table = lax.all_to_all(
            jnp.broadcast_to(ratio, (n_col,) + ratio.shape), "col", 0, 0, tiled=True
        )
        sent = pick(theirs, table)
        back = exchange(sent, both_places)
        done = backward(tab, records, back, est, hi, lo, sens, sweep, rows, cols)
        if sweep == 0:
            est, est2, sens = done
    return done[0]


def solution(mesh):
    in_specs = (
        P(None, "row", "col"),
        P("row", "col"),
        P(("row", "col"), None, None),
        P(("row", "col"), None, None),
        P("row", "col", None),
        P("row", "col"),
    )
    out_specs = P(None, "row", "col")
    return jax.shard_map(shards, mesh=mesh, in_specs=in_specs, out_specs=out_specs, check_vma=False)
```

```python
import functools
import jax
import jax.numpy as jnp
from jax import lax
from jax.experimental import pallas as pl
from jax.experimental.pallas import tpu as pltpu
from jax.sharding import PartitionSpec as P

ITERS = 2
LOG2E = 1.4426950408889634
CLUTTER_MAX = 1.5
BUILD_STEP = 4
BACK_STEP = 8
CHUNK = 512
STORE = 65536.0
INV_MAX = 1e37
SENS_ROWS = 16
LO_TYPE = jnp.float8_e5m2
BIG = 1e38
f32 = jnp.float32
bf16 = jnp.bfloat16


def split(x):
    hi = x.astype(bf16)
    return hi, (x - hi.astype(f32)).astype(bf16)


def wide_pair(x):
    top = lax.reduce_precision(x, 8, 7)
    pair = jnp.stack([top, x - top], axis=1)
    pair = jnp.pad(pair, ((0, 0), (0, 0), (0, 128 - x.shape[1])))
    return pair.reshape(x.shape[0], 256).astype(bf16)


def antenna_scale(record):
    peak = jnp.exp2(jnp.maximum(record[4:5, :] * (-LOG2E * CLUTTER_MAX), 0.0))
    return record[3:4, :] * (peak * (1.0 / STORE))


def any_live(tab, first, count):
    live = tab[first] >= 0
    for k in range(1, count):
        live = jnp.logical_or(live, tab[first + k] >= 0)
    return live


def build_kernel(tab, origin, records, clut, est2, hi, lo, part, across, *, rows, cols):
    step = pl.program_id(0)

    live_step = any_live(tab, step * BUILD_STEP // BACK_STEP * BACK_STEP, BACK_STEP)

    @pl.when(live_step)
    def _():
        for k in range(BUILD_STEP):
            block = tab[step * BUILD_STEP + k]
            live = block >= 0
            record = records[jnp.maximum(block, 0)]
            slope = jnp.where(live, record[4:5, :] * (-LOG2E), 0.0)
            peak = jnp.exp2(jnp.maximum(slope * CLUTTER_MAX, 0.0)) * (1.0 / STORE)
            inv = jnp.minimum(1.0 / (record[2:3, :] * record[2:3, :]), INV_MAX) * peak
            inv = jnp.where(live, inv, 0.0)
            peak = jnp.where(live, peak, jnp.inf)
            down = (
                origin[0] + lax.broadcasted_iota(jnp.int32, (rows, 128), 0)
            ).astype(f32) + (0.5 - record[0:1, :])
            down = peak + down * down * inv
            stack = [down, inv, record[1:2, :], slope, jnp.zeros((125 - rows, 128), f32)]
            turned = jnp.concatenate(stack, axis=0).T
            column = (
                origin[1] + lax.broadcasted_iota(jnp.int32, (1, cols), 1)
            ).astype(f32) + 0.5
            gap = column - turned[:, rows + 1 : rows + 2]
            across[k] = gap * gap * turned[:, rows : rows + 1]
            size = 32
            for a in range(0, 128, size):
                tilt = jnp.broadcast_to(turned[a : a + size, rows + 2 : rows + 3], (size, cols))
                side = across[k, a : a + size, :]
                at = slice(k * 128 + a, k * 128 + a + size)
                for r in range(rows):
                    den = side + turned[a : a + size, r : r + 1]
                    value = jnp.exp2(clut[r : r + 1, :] * tilt) / den
                    top = value.astype(bf16)
                    hi[at, r * cols : (r + 1) * cols] = top
                    lo[at, r * cols : (r + 1) * cols] = (value - top.astype(f32)).astype(LO_TYPE)
        forward_dot(tab, step, records, est2, hi, part)


def forward_dot(tab, step, records, est2, hi, part):
    count, _, maps, _ = part.shape
    both = jnp.dot(hi[...], est2[...], preferred_element_type=f32)
    total = both[:, :128] + both[:, 128:]
    for k in range(count):
        scale = antenna_scale(records[jnp.maximum(tab[step * count + k], 0)])
        part[k, 0] = total[k * 128 : (k + 1) * 128, :].T[:maps, :] * scale


def backward_kernel(tab, records, ratios, est, hi, lo, *rest, sweep):
    step = pl.program_id(0)
    maps, n_pixels = est.shape
    if sweep == 0:
        est_out, sens_out, part, est2, acc = rest
        steps = pl.num_programs(0) // 2
    else:
        sens_in, est_out, acc = rest
        steps = pl.num_programs(0)
    own = jnp.where(step < steps, step, 2 * steps - 1 - step)
    live_step = any_live(tab, own * BACK_STEP, BACK_STEP)

    @pl.when(step == 0)
    def _():
        acc[...] = jnp.zeros_like(acc)

    @pl.when(jnp.logical_and(live_step, step < steps))
    def _():
        wide = []
        thin = []
        for k in range(BACK_STEP):
            block = tab[own * BACK_STEP + k]
            live = block >= 0
            scale = antenna_scale(records[jnp.maximum(block, 0)])
            stack = jnp.where(live, ratios[k, 0] * scale, 0.0)
            if sweep == 0:
                ones = jnp.where(live, jnp.broadcast_to(scale, (SENS_ROWS, 128)), 0.0)
                stack = jnp.concatenate([stack, ones], axis=0)
            top, remainder = split(stack)
            wide.append(jnp.concatenate([top, remainder], axis=0))
            thin.append(top)
        wide = jnp.concatenate(wide, axis=1)
        thin = jnp.concatenate(thin, axis=1)
        height = thin.shape[0]
        chunk = CHUNK
        for at in range(0, n_pixels, chunk):
            both = jnp.dot(wide, hi[:, at : at + chunk], preferred_element_type=f32)
            low = jnp.dot(thin, lo[:, at : at + chunk], preferred_element_type=f32)
            acc[:, at : at + chunk] += both[:height, :] + (both[height:, :] + low)

    @pl.when(step == steps - 1)
    def _():
        if sweep == 0:
            sens = acc[maps : maps + 1, :]
            sens_out[...] = jnp.broadcast_to(sens, sens_out.shape)
            new = est[...] * acc[:maps, :] / sens
            est_out[...] = new
            turned = jnp.concatenate([new, jnp.zeros((128 - maps, n_pixels), f32)], axis=0).T
            top, remainder = split(turned)
            est2[:, :128] = top
            est2[:, 128:] = remainder
        else:
            rows, cols = est_out.shape[1:]
            for r in range(rows):
                at = slice(r * cols, (r + 1) * cols)
                est_out[:, r, :] = est[:, at] * acc[:maps, at] / sens_in[0:1, at]

    if sweep == 0:

        @pl.when(jnp.logical_and(live_step, step >= steps))
        def _():
            forward_dot(tab, own, records, est2, hi, part)


def combine_kernel(tab, recv, out):
    groups = recv.shape[0]
    out[...] = jnp.zeros_like(out)

    @pl.loop(0, groups)
    def _(i):
        for j in range(2):
            local = tab[j * groups + i]

            @pl.when(local >= 0)
            def _():
                out[local] = out[local] + recv[i, j]


def pick_kernel(tab, table, out):
    groups = out.shape[0]

    @pl.loop(0, groups)
    def _(i):
        for j in range(2):
            out[i, j] = table[jnp.maximum(tab[j * groups + i], 0)]


def params(mib):
    return pltpu.CompilerParams(vmem_limit_bytes=mib << 20)


def spec(shape, index):
    return pl.BlockSpec(shape, index)


def whole(shape):
    return pl.BlockSpec(shape, lambda *_: (0,) * len(shape))


def place_spec(slots, maps, step):
    per = slots // 2 // step
    return spec((step, 1, maps, 128), lambda i, *_: (i % per, i // per, 0, 0))


def build(tab, origin, records, clut, est2, maps, rows, cols):
    slots = tab.shape[0]
    n_pixels = rows * cols
    tall = BUILD_STEP * 128
    return pl.pallas_call(
        functools.partial(build_kernel, rows=rows, cols=cols),
        grid_spec=pltpu.PrefetchScalarGridSpec(
            num_scalar_prefetch=2,
            grid=(slots // BUILD_STEP,),
            in_specs=[whole(records.shape), whole(clut.shape), whole(est2.shape)],
            out_specs=[
                spec((tall, n_pixels), lambda i, *_: (i, 0)),
                spec((tall, n_pixels), lambda i, *_: (i, 0)),
                place_spec(slots, maps, BUILD_STEP),
            ],
            scratch_shapes=[pltpu.VMEM((BUILD_STEP, 128, cols), f32)],
        ),
        out_shape=[
            jax.ShapeDtypeStruct((slots * 128, n_pixels), bf16),
            jax.ShapeDtypeStruct((slots * 128, n_pixels), LO_TYPE),
            jax.ShapeDtypeStruct((slots // 2, 2, maps, 128), f32),
        ],
        compiler_params=params(56),
        name="build_cover",
    )(tab, origin, records, clut, est2)


def backward(tab, records, ratios, est, hi, lo, sens, sweep, rows, cols):
    slots = tab.shape[0]
    maps, n_pixels = est.shape
    tall = BACK_STEP * 128
    steps = slots // BACK_STEP
    per = slots // 2 // BACK_STEP
    height = maps + (SENS_ROWS if sweep == 0 else 0)

    def down(i):
        return jnp.minimum(i, steps - 1)

    def turn(i):
        return jnp.where(i < steps, i, 2 * steps - 1 - i)

    def up(i):
        return jnp.minimum(2 * steps - 1 - i, steps - 1)

    operands = [records, ratios, est, hi, lo]
    in_specs = [
        whole(records.shape),
        spec((BACK_STEP, 1, maps, 128), lambda i, *_: (down(i) % per, down(i) // per, 0, 0)),
        whole(est.shape),
        spec((tall, n_pixels), lambda i, *_: (turn(i), 0)),
        spec((tall, n_pixels), lambda i, *_: (down(i), 0)),
    ]
    scratch = [pltpu.VMEM((height, n_pixels), f32)]
    if sweep == 0:
        out_specs = [
            whole((maps, n_pixels)),
            whole((8, n_pixels)),
            spec((BACK_STEP, 1, maps, 128), lambda i, *_: (up(i) % per, up(i) // per, 0, 0)),
        ]
        out_shape = [
            jax.ShapeDtypeStruct((maps, n_pixels), f32),
            jax.ShapeDtypeStruct((8, n_pixels), f32),
            jax.ShapeDtypeStruct((slots // 2, 2, maps, 128), f32),
        ]
        scratch = [pltpu.VMEM((n_pixels, 256), bf16)] + scratch
    else:
        out_specs = [whole((maps, rows, cols))]
        out_shape = [jax.ShapeDtypeStruct((maps, rows, cols), f32)]
        operands.append(sens)
        in_specs.append(whole(sens.shape))
    return pl.pallas_call(
        functools.partial(backward_kernel, sweep=sweep),
        grid_spec=pltpu.PrefetchScalarGridSpec(
            num_scalar_prefetch=1,
            grid=((2 if sweep == 0 else 1) * steps,),
            in_specs=in_specs,
            out_specs=out_specs,
            scratch_shapes=scratch,
        ),
        out_shape=out_shape,
        compiler_params=params(56),
        name="backward_product",
    )(tab, *operands)


def combine(tab, recv, n_out):
    shape = (n_out,) + recv.shape[2:]
    return pl.pallas_call(
        combine_kernel,
        grid_spec=pltpu.PrefetchScalarGridSpec(
            num_scalar_prefetch=1,
            grid=(1,),
            in_specs=[whole(recv.shape)],
            out_specs=whole(shape),
        ),
        out_shape=jax.ShapeDtypeStruct(shape, f32),
        compiler_params=params(32),
        name="combine_slots",
    )(tab, recv)


def pick(tab, table):
    shape = (tab.shape[0] // 2, 2) + table.shape[1:]
    return pl.pallas_call(
        pick_kernel,
        grid_spec=pltpu.PrefetchScalarGridSpec(
            num_scalar_prefetch=1,
            grid=(1,),
            in_specs=[whole(table.shape)],
            out_specs=whole(shape),
        ),
        out_shape=jax.ShapeDtypeStruct(shape, f32),
        compiler_params=params(32),
        name="pick_slots",
    )(tab, table)


def slot_table(blocks, listed, n_groups, per_group):
    index = jnp.arange(blocks.shape[0], dtype=jnp.int32)
    group = jnp.where(index < listed, blocks // per_group, -1)
    same = (group[:, None] == group[None, :]) & (index[None, :] < index[:, None])
    place = jnp.sum(same.astype(jnp.int32), axis=1)
    key = jnp.where(group >= 0, place * n_groups + group, -1)
    hit = key[None, :] == jnp.arange(2 * n_groups, dtype=jnp.int32)[:, None]
    return jnp.sum(jnp.where(hit, blocks[None, :] + 1, 0), axis=1) - 1


def exchange(x, both_places):
    def first(x):
        got = lax.all_to_all(x[:, 0], "row", 0, 0, tiled=True)
        return jnp.stack([got, jnp.zeros_like(got)], axis=1)

    def full(x):
        return lax.all_to_all(x, "row", 0, 0, tiled=True)

    return lax.cond(both_places, full, first, x)


def shards(initial_estimate0, clutter, counts, antenna_settings, tile_block_list, tile_block_count):
    maps, rows, cols = initial_estimate0.shape
    n_pixels = rows * cols
    n_row = lax.axis_size("row")
    n_col = lax.axis_size("col")
    row = lax.axis_index("row")
    col = lax.axis_index("col")
    slots = tile_block_list.shape[2]

    record = jnp.pad(antenna_settings[0], ((0, 3), (0, 0)))
    mine = lax.all_to_all(jnp.broadcast_to(record, (n_col, 8, 128)), "col", 0, 0, tiled=True)
    tab = slot_table(tile_block_list.reshape(slots), tile_block_count.reshape(()), n_row, n_col)
    line = jnp.pad(tab.astype(f32), (0, 128 - 2 * n_row))
    mine, initial_estimate0 = lax.optimization_barrier((mine, initial_estimate0))
    here = lax.broadcasted_iota(jnp.int32, mine.shape, 1) == 5
    every = lax.all_to_all(
        jnp.broadcast_to(jnp.where(here, line, mine), (n_row, n_col, 8, 128)),
        "row",
        0,
        0,
        tiled=True,
    )
    records = every.reshape(n_row * n_col, 8, 128)
    tables = lax.dynamic_index_in_dim(every[:, :, 5, : 2 * n_row], col, 1, keepdims=False)
    tables = tables.astype(jnp.int32).reshape(n_row, 2, n_row)
    theirs = lax.dynamic_index_in_dim(tables, row, 2, keepdims=False)
    theirs = jnp.where(theirs >= 0, theirs - row * n_col, -1).T.reshape(2 * n_row)

    both_places = jnp.any(tables[:, 1] >= 0)
    origin = jnp.stack([row * rows, col * cols]).astype(jnp.int32)
    est = initial_estimate0.reshape(maps, n_pixels)
    est2 = wide_pair(initial_estimate0.transpose(1, 2, 0).reshape(n_pixels, maps))
    wanted = counts[0].astype(f32)

    hi, lo, part = build(tab, origin, records, clutter, est2, maps, rows, cols)
    sens = None
    for sweep in range(ITERS):
        group_sum = combine(theirs, exchange(part, both_places), n_col)
        pieces = lax.all_to_all(group_sum, "col", 0, 0, tiled=True)
        ratio = wanted / jnp.sum(pieces, axis=0)
        table = lax.all_to_all(
            jnp.broadcast_to(ratio, (n_col,) + ratio.shape), "col", 0, 0, tiled=True
        )
        sent = pick(theirs, table)
        back = exchange(sent, both_places)
        done = backward(tab, records, back, est, hi, lo, sens, sweep, rows, cols)
        if sweep == 0:
            est, sens, part = done
    return done[0]


def solution(mesh):
    in_specs = (
        P(None, "row", "col"),
        P("row", "col"),
        P(("row", "col"), None, None),
        P(("row", "col"), None, None),
        P("row", "col", None),
        P("row", "col"),
    )
    out_specs = P(None, "row", "col")
    return jax.shard_map(shards, mesh=mesh, in_specs=in_specs, out_specs=out_specs, check_vma=False)
```

```python
import functools
import jax
import jax.numpy as jnp
from jax import lax
from jax.experimental import pallas as pl
from jax.experimental.pallas import tpu as pltpu
from jax.sharding import PartitionSpec as P

ITERS = 2
LOG2E = 1.4426950408889634
CLUTTER_MAX = 1.5
BUILD_STEP = 4
BACK_STEP = 8
CHUNK = 512
STORE = 65536.0
INV_MAX = 1e37
SENS_ROWS = 16
LO_TYPE = jnp.float8_e5m2
BIG = 1e38
f32 = jnp.float32
bf16 = jnp.bfloat16


def split(x):
    hi = x.astype(bf16)
    return hi, (x - hi.astype(f32)).astype(bf16)


def wide_pair(x):
    top = lax.reduce_precision(x, 8, 7)
    pair = jnp.stack([top, x - top], axis=1)
    pair = jnp.pad(pair, ((0, 0), (0, 0), (0, 128 - x.shape[1])))
    return pair.reshape(x.shape[0], 256).astype(bf16)


def antenna_scale(record):
    peak = jnp.exp2(jnp.maximum(record[4:5, :] * (-LOG2E * CLUTTER_MAX), 0.0))
    return record[3:4, :] * (peak * (1.0 / STORE))


def any_live(tab, first, count):
    live = tab[first] >= 0
    for k in range(1, count):
        live = jnp.logical_or(live, tab[first + k] >= 0)
    return live


def build_kernel(tab, origin, records, clut, est2, hi, lo, part, across, *, rows, cols):
    step = pl.program_id(0)

    live_step = any_live(tab, step * BUILD_STEP // BACK_STEP * BACK_STEP, BACK_STEP)

    @pl.when(live_step)
    def _():
        for k in range(BUILD_STEP):
            block = tab[step * BUILD_STEP + k]
            live = block >= 0
            record = records[jnp.maximum(block, 0)]
            slope = jnp.where(live, record[4:5, :] * (-LOG2E), 0.0)
            peak = jnp.exp2(jnp.maximum(slope * CLUTTER_MAX, 0.0)) * (1.0 / STORE)
            inv = jnp.minimum(1.0 / (record[2:3, :] * record[2:3, :]), INV_MAX) * peak
            inv = jnp.where(live, inv, 0.0)
            peak = jnp.where(live, peak, jnp.inf)
            down = (
                origin[0] + lax.broadcasted_iota(jnp.int32, (rows, 128), 0)
            ).astype(f32) + (0.5 - record[0:1, :])
            down = peak + down * down * inv
            stack = [down, inv, record[1:2, :], slope, jnp.zeros((125 - rows, 128), f32)]
            turned = jnp.concatenate(stack, axis=0).T
            column = (
                origin[1] + lax.broadcasted_iota(jnp.int32, (1, cols), 1)
            ).astype(f32) + 0.5
            gap = column - turned[:, rows + 1 : rows + 2]
            across[k] = gap * gap * turned[:, rows : rows + 1]
            size = 32
            for a in range(0, 128, size):
                tilt = jnp.broadcast_to(turned[a : a + size, rows + 2 : rows + 3], (size, cols))
                side = across[k, a : a + size, :]
                at = slice(k * 128 + a, k * 128 + a + size)
                for r in range(rows):
                    den = side + turned[a : a + size, r : r + 1]
                    value = jnp.exp2(clut[r : r + 1, :] * tilt) / den
                    top = value.astype(bf16)
                    hi[at, r * cols : (r + 1) * cols] = top
                    lo[at, r * cols : (r + 1) * cols] = (value - top.astype(f32)).astype(LO_TYPE)
        forward_dot(tab, step, records, est2, hi, part)


def forward_dot(tab, step, records, est2, hi, part):
    count, _, maps, _ = part.shape
    both = jnp.dot(hi[...], est2[...], preferred_element_type=f32)
    total = both[:, :128] + both[:, 128:]
    for k in range(count):
        scale = antenna_scale(records[jnp.maximum(tab[step * count + k], 0)])
        part[k, 0] = total[k * 128 : (k + 1) * 128, :].T[:maps, :] * scale


def backward_kernel(tab, records, ratios, est, hi, lo, *rest, sweep):
    step = pl.program_id(0)
    maps, n_pixels = est.shape
    if sweep == 0:
        est_out, sens_out, part, est2, acc = rest
        steps = pl.num_programs(0) // 2
    else:
        sens_in, est_out, acc = rest
        steps = pl.num_programs(0)
    own = jnp.where(step < steps, step, 2 * steps - 1 - step)
    live_step = any_live(tab, own * BACK_STEP, BACK_STEP)

    @pl.when(step == 0)
    def _():
        acc[...] = jnp.zeros_like(acc)

    @pl.when(jnp.logical_and(live_step, step < steps))
    def _():
        wide = []
        thin = []
        for k in range(BACK_STEP):
            block = tab[own * BACK_STEP + k]
            live = block >= 0
            scale = antenna_scale(records[jnp.maximum(block, 0)])
            stack = jnp.where(live, ratios[k, 0] * scale, 0.0)
            if sweep == 0:
                ones = jnp.where(live, jnp.broadcast_to(scale, (SENS_ROWS, 128)), 0.0)
                stack = jnp.concatenate([stack, ones], axis=0)
            top, remainder = split(stack)
            wide.append(jnp.concatenate([top, remainder], axis=0))
            thin.append(top)
        wide = jnp.concatenate(wide, axis=1)
        thin = jnp.concatenate(thin, axis=1)
        height = thin.shape[0]
        chunk = CHUNK
        for at in range(0, n_pixels, chunk):
            both = jnp.dot(wide, hi[:, at : at + chunk], preferred_element_type=f32)
            low = jnp.dot(thin, lo[:, at : at + chunk], preferred_element_type=f32)
            acc[:, at : at + chunk] += both[:height, :] + (both[height:, :] + low)

    @pl.when(step == steps - 1)
    def _():
        if sweep == 0:
            sens = acc[maps : maps + 1, :]
            sens_out[...] = jnp.broadcast_to(sens, sens_out.shape)
            new = est[...] * acc[:maps, :] / sens
            est_out[...] = new
            turned = jnp.concatenate([new, jnp.zeros((128 - maps, n_pixels), f32)], axis=0).T
            top, remainder = split(turned)
            est2[:, :128] = top
            est2[:, 128:] = remainder
        else:
            rows, cols = est_out.shape[1:]
            for r in range(rows):
                at = slice(r * cols, (r + 1) * cols)
                est_out[:, r, :] = est[:, at] * acc[:maps, at] / sens_in[0:1, at]

    if sweep == 0:

        @pl.when(jnp.logical_and(live_step, step >= steps))
        def _():
            forward_dot(tab, own, records, est2, hi, part)


def combine_kernel(tab, recv, out):
    groups = recv.shape[0]
    out[...] = jnp.zeros_like(out)

    @pl.loop(0, groups)
    def _(i):
        for j in range(2):
            local = tab[j * groups + i]

            @pl.when(local >= 0)
            def _():
                out[local] = out[local] + recv[i, j]


def pick_kernel(tab, table, out):
    groups = out.shape[0]

    @pl.loop(0, groups)
    def _(i):
        for j in range(2):
            out[i, j] = table[jnp.maximum(tab[j * groups + i], 0)]


def params(mib):
    return pltpu.CompilerParams(vmem_limit_bytes=mib << 20)


def spec(shape, index):
    return pl.BlockSpec(shape, index)


def whole(shape):
    return pl.BlockSpec(shape, lambda *_: (0,) * len(shape))


def place_spec(slots, maps, step):
    per = slots // 2 // step
    return spec((step, 1, maps, 128), lambda i, *_: (i % per, i // per, 0, 0))


def build(tab, origin, records, clut, est2, maps, rows, cols):
    slots = tab.shape[0]
    n_pixels = rows * cols
    tall = BUILD_STEP * 128
    return pl.pallas_call(
        functools.partial(build_kernel, rows=rows, cols=cols),
        grid_spec=pltpu.PrefetchScalarGridSpec(
            num_scalar_prefetch=2,
            grid=(slots // BUILD_STEP,),
            in_specs=[whole(records.shape), whole(clut.shape), whole(est2.shape)],
            out_specs=[
                spec((tall, n_pixels), lambda i, *_: (i, 0)),
                spec((tall, n_pixels), lambda i, *_: (i, 0)),
                place_spec(slots, maps, BUILD_STEP),
            ],
            scratch_shapes=[pltpu.VMEM((BUILD_STEP, 128, cols), f32)],
        ),
        out_shape=[
            jax.ShapeDtypeStruct((slots * 128, n_pixels), bf16),
            jax.ShapeDtypeStruct((slots * 128, n_pixels), LO_TYPE),
            jax.ShapeDtypeStruct((slots // 2, 2, maps, 128), f32),
        ],
        compiler_params=params(56),
        name="build_cover",
    )(tab, origin, records, clut, est2)


def backward(tab, records, ratios, est, hi, lo, sens, sweep, rows, cols):
    slots = tab.shape[0]
    maps, n_pixels = est.shape
    tall = BACK_STEP * 128
    steps = slots // BACK_STEP
    per = slots // 2 // BACK_STEP
    second = jnp.any(tab[slots // 2 :] >= 0)
    used = jnp.where(second, steps, steps // 2).astype(jnp.int32)
    tab = jnp.concatenate([tab, used.reshape(1)])
    height = maps + (SENS_ROWS if sweep == 0 else 0)

    def down(i):
        return jnp.minimum(i, steps - 1)

    def turn(i):
        return jnp.where(i < steps, i, 2 * steps - 1 - i)

    def up(i):
        return jnp.minimum(2 * steps - 1 - i, steps - 1)

    operands = [records, ratios, est, hi, lo]
    in_specs = [
        whole(records.shape),
        spec((BACK_STEP, 1, maps, 128), lambda i, *_: (down(i) % per, down(i) // per, 0, 0)),
        whole(est.shape),
        spec((tall, n_pixels), lambda i, tab: (jnp.minimum(turn(i), tab[slots] - 1), 0)),
        spec((tall, n_pixels), lambda i, tab: (jnp.minimum(down(i), tab[slots] - 1), 0)),
    ]
    scratch = [pltpu.VMEM((height, n_pixels), f32)]
    if sweep == 0:
        out_specs = [
            whole((maps, n_pixels)),
            whole((8, n_pixels)),
            spec((BACK_STEP, 1, maps, 128), lambda i, *_: (up(i) % per, up(i) // per, 0, 0)),
        ]
        out_shape = [
            jax.ShapeDtypeStruct((maps, n_pixels), f32),
            jax.ShapeDtypeStruct((8, n_pixels), f32),
            jax.ShapeDtypeStruct((slots // 2, 2, maps, 128), f32),
        ]
        scratch = [pltpu.VMEM((n_pixels, 256), bf16)] + scratch
    else:
        out_specs = [whole((maps, rows, cols))]
        out_shape = [jax.ShapeDtypeStruct((maps, rows, cols), f32)]
        operands.append(sens)
        in_specs.append(whole(sens.shape))
    return pl.pallas_call(
        functools.partial(backward_kernel, sweep=sweep),
        grid_spec=pltpu.PrefetchScalarGridSpec(
            num_scalar_prefetch=1,
            grid=((2 if sweep == 0 else 1) * steps,),
            in_specs=in_specs,
            out_specs=out_specs,
            scratch_shapes=scratch,
        ),
        out_shape=out_shape,
        compiler_params=params(56),
        name="backward_product",
    )(tab, *operands)


def combine(tab, recv, n_out):
    shape = (n_out,) + recv.shape[2:]
    return pl.pallas_call(
        combine_kernel,
        grid_spec=pltpu.PrefetchScalarGridSpec(
            num_scalar_prefetch=1,
            grid=(1,),
            in_specs=[whole(recv.shape)],
            out_specs=whole(shape),
        ),
        out_shape=jax.ShapeDtypeStruct(shape, f32),
        compiler_params=params(32),
        name="combine_slots",
    )(tab, recv)


def pick(tab, table):
    shape = (tab.shape[0] // 2, 2) + table.shape[1:]
    return pl.pallas_call(
        pick_kernel,
        grid_spec=pltpu.PrefetchScalarGridSpec(
            num_scalar_prefetch=1,
            grid=(1,),
            in_specs=[whole(table.shape)],
            out_specs=whole(shape),
        ),
        out_shape=jax.ShapeDtypeStruct(shape, f32),
        compiler_params=params(32),
        name="pick_slots",
    )(tab, table)


def slot_table(blocks, listed, n_groups, per_group):
    index = jnp.arange(blocks.shape[0], dtype=jnp.int32)
    group = jnp.where(index < listed, blocks // per_group, -1)
    same = (group[:, None] == group[None, :]) & (index[None, :] < index[:, None])
    place = jnp.sum(same.astype(jnp.int32), axis=1)
    key = jnp.where(group >= 0, place * n_groups + group, -1)
    hit = key[None, :] == jnp.arange(2 * n_groups, dtype=jnp.int32)[:, None]
    return jnp.sum(jnp.where(hit, blocks[None, :] + 1, 0), axis=1) - 1


def exchange(x, both_places, cuts):
    def first(x):
        size = x.shape[2] // cuts
        got = [
            lax.all_to_all(x[:, 0, c * size : (c + 1) * size], "row", 0, 0, tiled=True)
            for c in range(cuts)
        ]
        got = jnp.concatenate(got, axis=1)
        return jnp.stack([got, jnp.zeros_like(got)], axis=1)

    def full(x):
        return lax.all_to_all(x, "row", 0, 0, tiled=True)

    return lax.cond(both_places, full, first, x)


def shards(initial_estimate0, clutter, counts, antenna_settings, tile_block_list, tile_block_count):
    maps, rows, cols = initial_estimate0.shape
    n_pixels = rows * cols
    n_row = lax.axis_size("row")
    n_col = lax.axis_size("col")
    row = lax.axis_index("row")
    col = lax.axis_index("col")
    slots = tile_block_list.shape[2]

    record = jnp.pad(antenna_settings[0], ((0, 3), (0, 0)))
    mine = lax.all_to_all(jnp.broadcast_to(record, (n_col, 8, 128)), "col", 0, 0, tiled=True)
    tab = slot_table(tile_block_list.reshape(slots), tile_block_count.reshape(()), n_row, n_col)
    line = jnp.pad(tab.astype(f32), (0, 128 - 2 * n_row))
    mine, initial_estimate0 = lax.optimization_barrier((mine, initial_estimate0))
    here = lax.broadcasted_iota(jnp.int32, mine.shape, 1) == 5
    every = lax.all_to_all(
        jnp.broadcast_to(jnp.where(here, line, mine), (n_row, n_col, 8, 128)),
        "row",
        0,
        0,
        tiled=True,
    )
    records = every.reshape(n_row * n_col, 8, 128)
    tables = lax.dynamic_index_in_dim(every[:, :, 5, : 2 * n_row], col, 1, keepdims=False)
    tables = tables.astype(jnp.int32).reshape(n_row, 2, n_row)
    theirs = lax.dynamic_index_in_dim(tables, row, 2, keepdims=False)
    theirs = jnp.where(theirs >= 0, theirs - row * n_col, -1).T.reshape(2 * n_row)

    both_places = jnp.any(tables[:, 1] >= 0)
    origin = jnp.stack([row * rows, col * cols]).astype(jnp.int32)
    est = initial_estimate0.reshape(maps, n_pixels)
    est2 = wide_pair(initial_estimate0.transpose(1, 2, 0).reshape(n_pixels, maps))
    wanted = counts[0].astype(f32)

    hi, lo, part = build(tab, origin, records, clutter, est2, maps, rows, cols)
    sens = None
    for sweep in range(ITERS):
        group_sum = combine(theirs, exchange(part, both_places, 1), n_col)
        pieces = lax.all_to_all(group_sum, "col", 0, 0, tiled=True)
        ratio = wanted / jnp.sum(pieces, axis=0)
        table = lax.all_to_all(
            jnp.broadcast_to(ratio, (n_col,) + ratio.shape), "col", 0, 0, tiled=True
        )
        sent = pick(theirs, table)
        back = exchange(sent, both_places, 2)
        done = backward(tab, records, back, est, hi, lo, sens, sweep, rows, cols)
        if sweep == 0:
            est, sens, part = done
    return done[0]


def solution(mesh):
    in_specs = (
        P(None, "row", "col"),
        P("row", "col"),
        P(("row", "col"), None, None),
        P(("row", "col"), None, None),
        P("row", "col", None),
        P("row", "col"),
    )
    out_specs = P(None, "row", "col")
    return jax.shard_map(shards, mesh=mesh, in_specs=in_specs, out_specs=out_specs, check_vma=False)
```

```python
import functools
import jax
import jax.numpy as jnp
from jax import lax
from jax.experimental import pallas as pl
from jax.experimental.pallas import tpu as pltpu
from jax.sharding import PartitionSpec as P

ITERS = 2
LOG2E = 1.4426950408889634
CLUTTER_MAX = 1.5
BUILD_STEP = 4
BACK_STEP = 8
CHUNK = 2048
STORE = 65536.0
INV_MAX = 1e37
SENS_ROWS = 16
LO_TYPE = jnp.float8_e5m2
BIG = 1e38
f32 = jnp.float32
bf16 = jnp.bfloat16


def split(x):
    hi = x.astype(bf16)
    return hi, (x - hi.astype(f32)).astype(bf16)


def wide_pair(x):
    top = lax.reduce_precision(x, 8, 7)
    pair = jnp.stack([top, x - top], axis=1)
    pair = jnp.pad(pair, ((0, 0), (0, 0), (0, 128 - x.shape[1])))
    return pair.reshape(x.shape[0], 256).astype(bf16)


def antenna_scale(record):
    peak = jnp.exp2(jnp.maximum(record[4:5, :] * (-LOG2E * CLUTTER_MAX), 0.0))
    return record[3:4, :] * (peak * (1.0 / STORE))


def any_live(tab, first, count):
    live = tab[first] >= 0
    for k in range(1, count):
        live = jnp.logical_or(live, tab[first + k] >= 0)
    return live


def build_kernel(tab, origin, records, clut, est2, hi, lo, part, across, *, rows, cols):
    step = pl.program_id(0)

    live_step = any_live(tab, step * BUILD_STEP // BACK_STEP * BACK_STEP, BACK_STEP)

    @pl.when(live_step)
    def _():
        for k in range(BUILD_STEP):
            block = tab[step * BUILD_STEP + k]
            live = block >= 0
            record = records[jnp.maximum(block, 0)]
            slope = jnp.where(live, record[4:5, :] * (-LOG2E), 0.0)
            peak = jnp.exp2(jnp.maximum(slope * CLUTTER_MAX, 0.0)) * (1.0 / STORE)
            inv = jnp.minimum(1.0 / (record[2:3, :] * record[2:3, :]), INV_MAX) * peak
            inv = jnp.where(live, inv, 0.0)
            peak = jnp.where(live, peak, jnp.inf)
            down = (
                origin[0] + lax.broadcasted_iota(jnp.int32, (rows, 128), 0)
            ).astype(f32) + (0.5 - record[0:1, :])
            down = peak + down * down * inv
            stack = [down, inv, record[1:2, :], slope, jnp.zeros((125 - rows, 128), f32)]
            turned = jnp.concatenate(stack, axis=0).T
            column = (
                origin[1] + lax.broadcasted_iota(jnp.int32, (1, cols), 1)
            ).astype(f32) + 0.5
            gap = column - turned[:, rows + 1 : rows + 2]
            across[k] = gap * gap * turned[:, rows : rows + 1]
            size = 32
            for a in range(0, 128, size):
                tilt = jnp.broadcast_to(turned[a : a + size, rows + 2 : rows + 3], (size, cols))
                side = across[k, a : a + size, :]
                at = slice(k * 128 + a, k * 128 + a + size)
                for r in range(rows):
                    den = side + turned[a : a + size, r : r + 1]
                    value = jnp.exp2(clut[r : r + 1, :] * tilt) / den
                    top = value.astype(bf16)
                    hi[at, r * cols : (r + 1) * cols] = top
                    lo[at, r * cols : (r + 1) * cols] = (value - top.astype(f32)).astype(LO_TYPE)
        forward_dot(tab, step, records, est2, hi, part)


def forward_dot(tab, step, records, est2, hi, part):
    count, _, maps, _ = part.shape
    both = jnp.dot(hi[...], est2[...], preferred_element_type=f32)
    total = both[:, :128] + both[:, 128:]
    for k in range(count):
        scale = antenna_scale(records[jnp.maximum(tab[step * count + k], 0)])
        part[k, 0] = total[k * 128 : (k + 1) * 128, :].T[:maps, :] * scale


def backward_kernel(tab, records, ratios, est, hi, lo, *rest, sweep):
    step = pl.program_id(0)
    maps, n_pixels = est.shape
    if sweep == 0:
        est_out, sens_out, part, est2, acc = rest
        steps = pl.num_programs(0) // 2
    else:
        sens_in, est_out, acc = rest
        steps = pl.num_programs(0)
    own = jnp.where(step < steps, step, 2 * steps - 1 - step)
    live_step = any_live(tab, own * BACK_STEP, BACK_STEP)

    @pl.when(step == 0)
    def _():
        acc[...] = jnp.zeros_like(acc)

    @pl.when(jnp.logical_and(live_step, step < steps))
    def _():
        wide = []
        thin = []
        for k in range(BACK_STEP):
            block = tab[own * BACK_STEP + k]
            live = block >= 0
            scale = antenna_scale(records[jnp.maximum(block, 0)])
            stack = jnp.where(live, ratios[k, 0] * scale, 0.0)
            if sweep == 0:
                ones = jnp.where(live, jnp.broadcast_to(scale, (SENS_ROWS, 128)), 0.0)
                stack = jnp.concatenate([stack, ones], axis=0)
            top, remainder = split(stack)
            wide.append(jnp.concatenate([top, remainder], axis=0))
            thin.append(top)
        wide = jnp.concatenate(wide, axis=1)
        thin = jnp.concatenate(thin, axis=1)
        height = thin.shape[0]
        chunk = CHUNK
        for at in range(0, n_pixels, chunk):
            both = jnp.dot(wide, hi[:, at : at + chunk], preferred_element_type=f32)
            low = jnp.dot(thin, lo[:, at : at + chunk], preferred_element_type=f32)
            acc[:, at : at + chunk] += both[:height, :] + (both[height:, :] + low)

    @pl.when(step == steps - 1)
    def _():
        if sweep == 0:
            sens = acc[maps : maps + 1, :]
            sens_out[...] = jnp.broadcast_to(sens, sens_out.shape)
            new = est[...] * acc[:maps, :] / sens
            est_out[...] = new
            turned = jnp.concatenate([new, jnp.zeros((128 - maps, n_pixels), f32)], axis=0).T
            top, remainder = split(turned)
            est2[:, :128] = top
            est2[:, 128:] = remainder
        else:
            rows, cols = est_out.shape[1:]
            for r in range(rows):
                at = slice(r * cols, (r + 1) * cols)
                est_out[:, r, :] = est[:, at] * acc[:maps, at] / sens_in[0:1, at]

    if sweep == 0:

        @pl.when(jnp.logical_and(live_step, step >= steps))
        def _():
            forward_dot(tab, own, records, est2, hi, part)


def combine_kernel(tab, recv, out):
    groups = recv.shape[0]
    out[...] = jnp.zeros_like(out)

    @pl.loop(0, groups)
    def _(i):
        for j in range(2):
            local = tab[j * groups + i]

            @pl.when(local >= 0)
            def _():
                out[local] = out[local] + recv[i, j]


def pick_kernel(tab, table, out):
    groups = out.shape[0]

    @pl.loop(0, groups)
    def _(i):
        for j in range(2):
            out[i, j] = table[jnp.maximum(tab[j * groups + i], 0)]


def params(mib):
    return pltpu.CompilerParams(vmem_limit_bytes=mib << 20)


def spec(shape, index):
    return pl.BlockSpec(shape, index)


def whole(shape):
    return pl.BlockSpec(shape, lambda *_: (0,) * len(shape))


def place_spec(slots, maps, step):
    per = slots // 2 // step
    return spec((step, 1, maps, 128), lambda i, *_: (i % per, i // per, 0, 0))


def build(tab, origin, records, clut, est2, maps, rows, cols):
    slots = tab.shape[0]
    n_pixels = rows * cols
    tall = BUILD_STEP * 128
    return pl.pallas_call(
        functools.partial(build_kernel, rows=rows, cols=cols),
        grid_spec=pltpu.PrefetchScalarGridSpec(
            num_scalar_prefetch=2,
            grid=(slots // BUILD_STEP,),
            in_specs=[whole(records.shape), whole(clut.shape), whole(est2.shape)],
            out_specs=[
                spec((tall, n_pixels), lambda i, *_: (i, 0)),
                spec((tall, n_pixels), lambda i, *_: (i, 0)),
                place_spec(slots, maps, BUILD_STEP),
            ],
            scratch_shapes=[pltpu.VMEM((BUILD_STEP, 128, cols), f32)],
        ),
        out_shape=[
            jax.ShapeDtypeStruct((slots * 128, n_pixels), bf16),
            jax.ShapeDtypeStruct((slots * 128, n_pixels), LO_TYPE),
            jax.ShapeDtypeStruct((slots // 2, 2, maps, 128), f32),
        ],
        compiler_params=params(56),
        name="build_cover",
    )(tab, origin, records, clut, est2)


def backward(tab, records, ratios, est, hi, lo, sens, sweep, rows, cols):
    slots = tab.shape[0]
    maps, n_pixels = est.shape
    tall = BACK_STEP * 128
    steps = slots // BACK_STEP
    per = slots // 2 // BACK_STEP
    second = jnp.any(tab[slots // 2 :] >= 0)
    used = jnp.where(second, steps, steps // 2).astype(jnp.int32)
    tab = jnp.concatenate([tab, used.reshape(1)])
    height = maps + (SENS_ROWS if sweep == 0 else 0)

    def down(i):
        return jnp.minimum(i, steps - 1)

    def turn(i):
        return jnp.where(i < steps, i, 2 * steps - 1 - i)

    def up(i):
        return jnp.minimum(2 * steps - 1 - i, steps - 1)

    operands = [records, ratios, est, hi, lo]
    in_specs = [
        whole(records.shape),
        spec((BACK_STEP, 1, maps, 128), lambda i, *_: (down(i) % per, down(i) // per, 0, 0)),
        whole(est.shape),
        spec((tall, n_pixels), lambda i, tab: (jnp.minimum(turn(i), tab[slots] - 1), 0)),
        spec((tall, n_pixels), lambda i, tab: (jnp.minimum(down(i), tab[slots] - 1), 0)),
    ]
    scratch = [pltpu.VMEM((height, n_pixels), f32)]
    if sweep == 0:
        out_specs = [
            whole((maps, n_pixels)),
            whole((8, n_pixels)),
            spec((BACK_STEP, 1, maps, 128), lambda i, *_: (up(i) % per, up(i) // per, 0, 0)),
        ]
        out_shape = [
            jax.ShapeDtypeStruct((maps, n_pixels), f32),
            jax.ShapeDtypeStruct((8, n_pixels), f32),
            jax.ShapeDtypeStruct((slots // 2, 2, maps, 128), f32),
        ]
        scratch = [pltpu.VMEM((n_pixels, 256), bf16)] + scratch
    else:
        out_specs = [whole((maps, rows, cols))]
        out_shape = [jax.ShapeDtypeStruct((maps, rows, cols), f32)]
        operands.append(sens)
        in_specs.append(whole(sens.shape))
    return pl.pallas_call(
        functools.partial(backward_kernel, sweep=sweep),
        grid_spec=pltpu.PrefetchScalarGridSpec(
            num_scalar_prefetch=1,
            grid=((2 if sweep == 0 else 1) * steps,),
            in_specs=in_specs,
            out_specs=out_specs,
            scratch_shapes=scratch,
        ),
        out_shape=out_shape,
        compiler_params=params(56),
        name="backward_product",
    )(tab, *operands)


def combine(tab, recv, n_out):
    shape = (n_out,) + recv.shape[2:]
    return pl.pallas_call(
        combine_kernel,
        grid_spec=pltpu.PrefetchScalarGridSpec(
            num_scalar_prefetch=1,
            grid=(1,),
            in_specs=[whole(recv.shape)],
            out_specs=whole(shape),
        ),
        out_shape=jax.ShapeDtypeStruct(shape, f32),
        compiler_params=params(32),
        name="combine_slots",
    )(tab, recv)


def pick(tab, table):
    shape = (tab.shape[0] // 2, 2) + table.shape[1:]
    return pl.pallas_call(
        pick_kernel,
        grid_spec=pltpu.PrefetchScalarGridSpec(
            num_scalar_prefetch=1,
            grid=(1,),
            in_specs=[whole(table.shape)],
            out_specs=whole(shape),
        ),
        out_shape=jax.ShapeDtypeStruct(shape, f32),
        compiler_params=params(32),
        name="pick_slots",
    )(tab, table)


def slot_table(blocks, listed, n_groups, per_group):
    index = jnp.arange(blocks.shape[0], dtype=jnp.int32)
    group = jnp.where(index < listed, blocks // per_group, -1)
    same = (group[:, None] == group[None, :]) & (index[None, :] < index[:, None])
    place = jnp.sum(same.astype(jnp.int32), axis=1)
    key = jnp.where(group >= 0, place * n_groups + group, -1)
    hit = key[None, :] == jnp.arange(2 * n_groups, dtype=jnp.int32)[:, None]
    return jnp.sum(jnp.where(hit, blocks[None, :] + 1, 0), axis=1) - 1


def exchange(x, both_places, cuts):
    def first(x):
        size = x.shape[2] // cuts
        got = [
            lax.all_to_all(x[:, 0, c * size : (c + 1) * size], "row", 0, 0, tiled=True)
            for c in range(cuts)
        ]
        got = jnp.concatenate(got, axis=1)
        return jnp.stack([got, jnp.zeros_like(got)], axis=1)

    def full(x):
        return lax.all_to_all(x, "row", 0, 0, tiled=True)

    return lax.cond(both_places, full, first, x)


def shards(initial_estimate0, clutter, counts, antenna_settings, tile_block_list, tile_block_count):
    maps, rows, cols = initial_estimate0.shape
    n_pixels = rows * cols
    n_row = lax.axis_size("row")
    n_col = lax.axis_size("col")
    row = lax.axis_index("row")
    col = lax.axis_index("col")
    slots = tile_block_list.shape[2]

    record = jnp.pad(antenna_settings[0], ((0, 3), (0, 0)))
    mine = lax.all_to_all(jnp.broadcast_to(record, (n_col, 8, 128)), "col", 0, 0, tiled=True)
    tab = slot_table(tile_block_list.reshape(slots), tile_block_count.reshape(()), n_row, n_col)
    line = jnp.pad(tab.astype(f32), (0, 128 - 2 * n_row))
    mine, initial_estimate0 = lax.optimization_barrier((mine, initial_estimate0))
    here = lax.broadcasted_iota(jnp.int32, mine.shape, 1) == 5
    every = lax.all_to_all(
        jnp.broadcast_to(jnp.where(here, line, mine), (n_row, n_col, 8, 128)),
        "row",
        0,
        0,
        tiled=True,
    )
    records = every.reshape(n_row * n_col, 8, 128)
    tables = lax.dynamic_index_in_dim(every[:, :, 5, : 2 * n_row], col, 1, keepdims=False)
    tables = tables.astype(jnp.int32).reshape(n_row, 2, n_row)
    theirs = lax.dynamic_index_in_dim(tables, row, 2, keepdims=False)
    theirs = jnp.where(theirs >= 0, theirs - row * n_col, -1).T.reshape(2 * n_row)

    both_places = jnp.any(tables[:, 1] >= 0)
    origin = jnp.stack([row * rows, col * cols]).astype(jnp.int32)
    est = initial_estimate0.reshape(maps, n_pixels)
    est2 = wide_pair(initial_estimate0.transpose(1, 2, 0).reshape(n_pixels, maps))
    wanted = counts[0].astype(f32)

    hi, lo, part = build(tab, origin, records, clutter, est2, maps, rows, cols)
    sens = None
    for sweep in range(ITERS):
        group_sum = combine(theirs, exchange(part, both_places, 1), n_col)
        pieces = lax.all_to_all(group_sum, "col", 0, 0, tiled=True)
        ratio = wanted / jnp.sum(pieces, axis=0)
        table = lax.all_to_all(
            jnp.broadcast_to(ratio, (n_col,) + ratio.shape), "col", 0, 0, tiled=True
        )
        sent = pick(theirs, table)
        back = exchange(sent, both_places, 2)
        done = backward(tab, records, back, est, hi, lo, sens, sweep, rows, cols)
        if sweep == 0:
            est, sens, part = done
    return done[0]


def solution(mesh):
    in_specs = (
        P(None, "row", "col"),
        P("row", "col"),
        P(("row", "col"), None, None),
        P(("row", "col"), None, None),
        P("row", "col", None),
        P("row", "col"),
    )
    out_specs = P(None, "row", "col")
    return jax.shard_map(shards, mesh=mesh, in_specs=in_specs, out_specs=out_specs, check_vma=False)
```
